512 devices in a mesh: dom: 256 (over x_hi, y, z, core), band: 2 (over x_lo).
Axes of the slice: x: 4 (x_hi: 2, x_lo: 2; x = x_hi * 2 + x_lo), y: 8, z: 8, core: 2. Of those that a mesh axis runs over, the one named last changes fastest.
Arguments:
- orbitals: float32 [256, 16, 12, 16, 128], P('dom', 'band'), may hold values from -6 to 6
- potential: float32 [256, 12, 16, 128], P('dom'), may hold values from -12 to 4
- projectors: bfloat16 [65536, 4, 128], P('dom'), may hold values from -0.359375 to 0.359375
- entry_atom: int32 [65536], P('dom'), may hold values from 0 to 1023, as said below
- entry_block: int32 [65536], P('dom'), may hold values from 0 to 191
- kb_energy: float32 [1024, 4], replicated, may hold values from 1 to 10
- panel: bfloat16 [16, 16], replicated, may hold values from -1.5 to 1.5
Outputs:
- rotated: float32 [256, 16, 12, 16, 128], P('dom', 'band')
The draws below stay inside these ranges and needn't reach their ends.
Inputs may be any that keep to these rules, and one draw needn't show every extreme that they name: `entry_atom`: atom a is owned by domain a // 4; every entry of domain d belongs to an atom owned by d or by a domain that shares a face with d in the 8 x 8 x 4 arrangement of domains (no wrap-around).
All inputs are finite; a program needn't handle non-finite values.
Results may differ from the reference program's by a relative error of at most 0.00115.
The reference program's roundings to bfloat16 on the way (of `filtered`) count: a program that leaves them out, or rounds other values in their place, can miss the bound.
Values may be sent and summed in bfloat16 or wider, within the bound.
A program may use at most 64 MiB of HBM per device.

```python
import math
import jax
import jax.numpy as jnp
from jax import lax

NORB = 16
NPROJ = 4
RADIUS = 6
BLK = 128
CX = 12
CY = 16
CZ = 128
ENT = 256
ATOM_DEV = 4
DOM_Z = 4
DOM_Y = 8
DOM_X = 8
NX = 96
NY = 128
NZ = 512
ATOMS = 1024
NBLK = 192
N_DOM = 256


def draw_entry_atom(key, part):
    total = N_DOM * ENT
    domain = jnp.arange(total, dtype=jnp.int32) // ENT
    first = domain // (DOM_Y * DOM_Z)
    second = domain // DOM_Z % DOM_Y
    third = domain % DOM_Z
    key_dir = jax.random.fold_in(key, 11)
    key_loc = jax.random.fold_in(key, 23)
    direction = jax.random.randint(key_dir, (total,), 0, 7, dtype=jnp.int32)
    chosen = jax.random.randint(key_loc, (total,), 0, ATOM_DEV, dtype=jnp.int32)
    step_first = jnp.array([0, 1, -1, 0, 0, 0, 0], dtype=jnp.int32)[direction]
    step_second = jnp.array([0, 0, 0, 1, -1, 0, 0], dtype=jnp.int32)[direction]
    step_third = jnp.array([0, 0, 0, 0, 0, 1, -1], dtype=jnp.int32)[direction]
    new_first = first + step_first
    new_second = second + step_second
    new_third = third + step_third
    inside = (new_first >= 0) & (new_first < DOM_X) & (new_second >= 0) & (new_second < DOM_Y) & (new_third >= 0) & (new_third < DOM_Z)
    new_first = jnp.where(inside, new_first, first)
    new_second = jnp.where(inside, new_second, second)
    new_third = jnp.where(inside, new_third, third)
    owner = (new_first * DOM_Y + new_second) * DOM_Z + new_third
    return (owner * ATOM_DEV + chosen).astype(jnp.int32)


def draw_orbitals(key, part):
    shape = (N_DOM, NORB, CX, CY, CZ)
    domain = jnp.arange(N_DOM, dtype=jnp.int32)[:, None, None, None, None]
    first = domain // (DOM_Y * DOM_Z) * CX + jnp.arange(CX, dtype=jnp.int32)[None, None, :, None, None]
    second = domain // DOM_Z % DOM_Y * CY + jnp.arange(CY, dtype=jnp.int32)[None, None, None, :, None]
    third = domain % DOM_Z * CZ + jnp.arange(CZ, dtype=jnp.int32)[None, None, None, None, :]
    key_cycle = jax.random.fold_in(key, 31)
    key_phase = jax.random.fold_in(key, 37)
    key_rough = jax.random.fold_in(key, 41)
    cycles = jax.random.uniform(key_cycle, (3, NORB), jnp.float32, 0.5, 2.0)
    phases = jax.random.uniform(key_phase, (3, NORB), jnp.float32, -3.14159, 3.14159)

    def wave(coord, count, index):
        turns = coord.astype(jnp.float32) / float(count)
        angle = 6.2831853 * turns * cycles[index][None, :, None, None, None] + phases[index][None, :, None, None, None]
        return jnp.sin(angle)
    smooth = wave(first, NX, 0) + wave(second, NY, 1) + wave(third, NZ, 2)
    rough = 0.6 * jax.random.truncated_normal(key_rough, -3.0, 3.0, shape, jnp.float32)
    amplitude = 1.2
    return (amplitude * smooth + rough).astype(jnp.float32)


def touch_ends(values, stream_key, smallest, high):
    longest = values.shape.index(max(values.shape))
    spots = []
    for shift in (0, 1):
        where = [jax.random.randint(jax.random.fold_in(stream_key, axis), (), 0, length) for axis, length in enumerate(values.shape)]
        where[longest] = (where[longest] + shift) % values.shape[longest]
        spots.append(tuple(where))
    return values.at[spots[0]].set(smallest).at[spots[1]].set(high)


def block_scale(stream_key, dims, shards, least, largest):
    def one(axis_at, parts):
        draws = jax.random.uniform(jax.random.fold_in(jax.random.fold_in(stream_key, 6), axis_at), (parts,), jnp.float32, least / len(shards), largest / len(shards))
        return jnp.repeat(jnp.exp(draws), dims[axis_at] // parts).reshape((-1,) + (1,) * (len(dims) - axis_at - 1))

    level = one(*shards[0])
    for cut in shards[1:]:
        level = level * one(*cut)
    return level


def bell_draw(rng, shape, spread, limit, shards=(), kind=jnp.bfloat16):
    entries = spread * jax.random.normal(rng, shape, jnp.float32)
    if shards:
        entries = entries * block_scale(rng, shape, shards, -0.22, 0.18)
    return jnp.clip(entries, -limit, limit).astype(kind)


def setup_inputs(seed: int = 0) -> dict:
    key_of = jax.random.split(jax.random.key(seed), 8)
    orbitals = draw_orbitals(jax.random.fold_in(key_of[7], 71), 0)
    potential = jnp.clip(-12.0 + 16.0 * jax.random.uniform(key_of[1], (N_DOM, CX, CY, CZ), jnp.float32) ** block_scale(key_of[1], (N_DOM, CX, CY, CZ), ((0, 256),), -0.2, 0.2), -12.0, 4.0)
    projectors = bell_draw(key_of[2], (N_DOM * ENT, NPROJ, BLK), 0.06, 0.359375, ((0, 256),))
    entry_atom = draw_entry_atom(jax.random.fold_in(key_of[7], 71), 0)
    entry_block = touch_ends(jax.random.randint(key_of[4], (N_DOM * ENT,), 0, NBLK), jax.random.fold_in(key_of[4], 1), 0, NBLK - 1).astype(jnp.int32)
    kb_energy = jnp.clip(jnp.exp(jax.random.uniform(key_of[5], (ATOMS, NPROJ), jnp.float32, math.log(1.0), math.log(10.0))), 1.0, 10.0)
    panel = bell_draw(key_of[6], (NORB, NORB), NORB ** -0.5, 1.5)
    return {"orbitals": orbitals, "potential": potential, "projectors": projectors, "entry_atom": entry_atom, "entry_block": entry_block, "kb_energy": kb_energy, "panel": panel}


COEFFS = (-5369.0 / 1800.0, 12.0 / 7.0, -15.0 / 56.0, 10.0 / 189.0, -1.0 / 112.0, 2.0 / 1925.0, -1.0 / 16632.0)
KINETIC = -3.125
CENTER = 36.0
HALF_WIDTH = 34.0


def to_grid(blocks):
    shaped = blocks.reshape(DOM_X, DOM_Y, DOM_Z, CX, CY, CZ)
    return shaped.transpose(0, 3, 1, 4, 2, 5).reshape(NX, NY, NZ)


def to_blocks(grid_values):
    shaped = grid_values.reshape(DOM_X, CX, DOM_Y, CY, DOM_Z, CZ)
    return shaped.transpose(0, 2, 4, 1, 3, 5).reshape(N_DOM, CX, CY, CZ)


def window(padded, position, offset, extents):
    pieces = [slice(RADIUS, RADIUS + extents[0]), slice(RADIUS, RADIUS + extents[1]), slice(RADIUS, RADIUS + extents[2])]
    pieces[position] = slice(RADIUS + offset, RADIUS + offset + extents[position])
    return padded[tuple(pieces)]


def local_part(grid_values, pot_grid):
    padded = jnp.pad(grid_values, RADIUS)
    extents = grid_values.shape
    laplace = 3.0 * COEFFS[0] * grid_values
    for position in range(3):
        for offset in range(1, RADIUS + 1):
            upward = window(padded, position, offset, extents)
            downward = window(padded, position, -offset, extents)
            laplace = laplace + COEFFS[offset] * (upward + downward)
    return KINETIC * laplace + pot_grid * grid_values


def reference(orbitals, potential, projectors, entry_atom, entry_block, kb_energy, panel):
    pot_grid = to_grid(potential)
    proj_values = projectors.astype(jnp.float32)
    entry_domain = (jnp.arange(N_DOM * ENT, dtype=jnp.int32) // ENT).astype(jnp.int32)

    def nonlocal_part(grid_values):
        rows_all = to_blocks(grid_values).reshape(N_DOM, NBLK, BLK)
        picked = rows_all[entry_domain, entry_block]
        intersections = jnp.einsum('epk,ek->ep', proj_values, picked, precision=lax.Precision.HIGHEST)
        atom_table = jax.ops.segment_sum(intersections, entry_atom, num_segments=ATOMS)
        scaled = kb_energy * atom_table
        per_entry = scaled[entry_atom]
        additions = jnp.einsum('epk,ep->ek', proj_values, per_entry, precision=lax.Precision.HIGHEST)
        result = jnp.zeros((N_DOM, NBLK, BLK), jnp.float32).at[entry_domain, entry_block].add(additions)
        return to_grid(result.reshape(N_DOM, CX, CY, CZ))

    def apply_ham(grid_values):
        return local_part(grid_values, pot_grid) + nonlocal_part(grid_values)

    def filter_one(blocks):
        start_grid = to_grid(blocks)
        applied = apply_ham(start_grid)
        first_step = (applied - CENTER * start_grid) / HALF_WIDTH
        applied_again = apply_ham(first_step)
        second_step = 2.0 * (applied_again - CENTER * first_step) / HALF_WIDTH - start_grid
        return to_blocks(second_step).astype(jnp.bfloat16)

    filtered = lax.map(filter_one, jnp.transpose(orbitals, (1, 0, 2, 3, 4)))
    rotated = jnp.einsum('iabcd,ij->jabcd', filtered.astype(jnp.float32), panel.astype(jnp.float32), precision=lax.Precision.HIGHEST)
    return jnp.transpose(rotated, (1, 0, 2, 3, 4))
```

```python
import jax
import jax.numpy as jnp
import ml_dtypes
import numpy as np
from jax import lax
from jax.experimental import pallas as pl
from jax.experimental.pallas import tpu as pltpu
from jax.sharding import PartitionSpec as P

COEFFS = (
    -5369.0 / 1800.0,
    12.0 / 7.0,
    -15.0 / 56.0,
    10.0 / 189.0,
    -1.0 / 112.0,
    2.0 / 1925.0,
    -1.0 / 16632.0,
)
KINETIC = -3.125
CENTER = 36.0
HALF_WIDTH = 34.0
REACH = 6

DOM_Z = 4
DOM_Y = 8
NORB = 8
CX, CY, CZ = 12, 16, 128
ENT = 256
ROWS = CX * CY
HALF = ROWS // 2
OWNED = 4
CHUNK = 2
NCHUNK = NORB // CHUNK
GROUP = 4
NGROUP = NORB // GROUP
LANE_SLOT = 16
SCALE = 64 * 1.0937445
F32 = jnp.float32
BF16 = jnp.bfloat16
OPPOSITE = (1, 0, 3, 2, 5, 4)
NN = (((1,), (0,)), ((), ()))
NT = (((1,), (1,)), ((), ()))


def tap(distance):
    return SCALE * COEFFS[abs(distance)]


def stencil_tables():
    plane = np.zeros((ROWS, 8 * HALF), np.float32)
    for x in range(CX):
        for y in range(CY):
            row = y // 8 * HALF + x * 8 + y % 8
            for step in (s for s in range(-REACH, REACH + 1) if s):
                to = x + step
                if 0 <= to < CX:
                    near = y // 8 * HALF + to * 8 + y % 8
                    plane[row, near] += tap(step)
                    plane[row, 6 * HALF + near] += tap(step)
                else:
                    place = (to + REACH) * 8 if to < 0 else HALF // 2 + (to - CX) * 8
                    plane[row, (2 + y // 8) * HALF + place + y % 8] += tap(step)
                to = y + step
                if 0 <= to < CY:
                    near = to // 8 * HALF + x * 8 + to % 8
                    plane[row, near] += tap(step)
                    plane[row, 6 * HALF + near] += tap(step)
                elif to < 0:
                    plane[row, 4 * HALF + x * 8 + to + 8] += tap(step)
                else:
                    plane[row, 5 * HALF + x * 8 + to - CY] += tap(step)
    line = np.zeros((2 * CZ, CZ), np.float32)
    edge = np.zeros((NORB, 2 * CZ, CZ), np.float32)
    pack = np.zeros((NORB, CZ, 2 * CZ), np.float32)
    for z in range(CZ):
        for step in (s for s in range(-REACH, REACH + 1) if s):
            to = z + step
            for o in range(NORB):
                if to < 0:
                    edge[o, o * LANE_SLOT + to + REACH, z] = tap(step)
                elif to >= CZ:
                    edge[o, CZ + o * LANE_SLOT + to - CZ, z] = tap(step)
            if 0 <= to < CZ:
                line[to, z] = line[CZ + to, z] = tap(step)
    for o in range(NORB):
        for k in range(REACH):
            pack[o, k, o * LANE_SLOT + k] = 1.0
            pack[o, CZ - REACH + k, CZ + o * LANE_SLOT + k] = 1.0
    return [t.astype(ml_dtypes.bfloat16) for t in (plane, line, edge, pack)]


def dot(a, b, dims=NN):
    return lax.dot_general(a, b, dims, preferred_element_type=F32)


def iota(shape, axis):
    return lax.broadcasted_iota(jnp.int32, shape, axis)


def split(values):
    high = values.astype(BF16)
    return high, (values - high.astype(F32)).astype(BF16)


def kernel(
    orb_hbm, pot_hbm, proj_hbm, atom_ref, block_ref, energy_hbm, panel_ref, plane_hbm, line_hbm, edge_hbm, pack_hbm,
    out_hbm,
    start, field, first, weight, proj, energy, plane, line, edge, pack,
    z_out, z_in, filtered, partner, result,
    pick, spread, slots, picked, inner, additions, table_out, table_in, scaled_out, scaled_in, mix,
    local_sem, halo_send, halo_recv, table_send, table_recv, band_send, band_recv, out_sem,
):
    dom = lax.axis_index("dom")
    band = lax.axis_index("band")
    count = lax.axis_size("dom")
    plane_size = DOM_Y * DOM_Z
    at = (dom // plane_size, dom // DOM_Z % DOM_Y, dom % DOM_Z)
    extents = (count // plane_size, DOM_Y, DOM_Z)
    strides = (plane_size, -plane_size, DOM_Z, -DOM_Z, 1, -1)
    has = []
    for axis in range(3):
        has.append(at[axis] < extents[axis] - 1)
        has.append(at[axis] > 0)

    def toward(d):
        return {"dom": jnp.clip(dom + strides[d], 0, count - 1)}

    loads = []

    def load(src, dst):
        copy = pltpu.make_async_copy(src, dst, local_sem.at[len(loads)])
        copy.start()
        loads.append(copy)
        return copy

    orb_loads = [
        [
            load(
                orb_hbm.at[0, pl.ds(c * CHUNK, CHUNK), :, pl.ds(h * 8, 8), :],
                start.at[pl.ds(c * CHUNK, CHUNK), h],
            )
            for h in range(2)
        ]
        for c in range(NCHUNK)
    ]
    pack_load = load(pack_hbm, pack)
    proj_load = load(proj_hbm, proj)
    pot_loads = [load(pot_hbm.at[0, :, pl.ds(h * 8, 8), :], weight.at[h]) for h in range(2)]
    width = energy.shape[1]
    energy_load = load(energy_hbm.at[:, pl.ds(pl.multiple_of(dom * OWNED // width * width, width), width)], energy)
    plane_load = load(plane_hbm, plane)
    line_load = load(line_hbm, line)
    edge_load = load(edge_hbm, edge)

    barrier = pltpu.get_barrier_semaphore()
    partners = jnp.int32(1)
    for d in range(6):
        partners = partners + has[d].astype(jnp.int32)

        @pl.when(has[d])
        def _():
            pl.semaphore_signal(barrier, inc=1, device_id=toward(d), device_id_type=pl.DeviceIdType.MESH)

    pl.semaphore_signal(barrier, inc=1, device_id={"band": 1 - band}, device_id_type=pl.DeviceIdType.MESH)

    for h in range(2):
        for d in range(6):

            @pl.when(jnp.logical_not(has[OPPOSITE[d]]))
            def _():
                if d == 0:
                    field[h, :, 2:4, 0 : HALF // 2, :] = jnp.zeros((NORB, 2, HALF // 2, CZ), BF16)
                elif d == 1:
                    field[h, :, 2:4, HALF // 2 : HALF, :] = jnp.zeros((NORB, 2, HALF // 2, CZ), BF16)
                elif d == 2:
                    field[h, :, 4, :, :] = jnp.zeros((NORB, HALF, CZ), BF16)
                elif d == 3:
                    field[h, :, 5, :, :] = jnp.zeros((NORB, HALF, CZ), BF16)
                else:
                    z_in[h, :, d - 4] = jnp.zeros((NCHUNK, ROWS, CZ), BF16)
                table_in[h, :, d] = jnp.zeros((NGROUP, 8, CZ), F32)
                scaled_in[h, :, d] = jnp.zeros((NGROUP, 8, CZ), F32)

    table_out[...] = jnp.zeros(table_out.shape, F32)

    def halo(h, c, d):
        own = pl.ds(c * CHUNK, CHUNK)
        low, high = pl.ds(0, HALF // 2), pl.ds(HALF // 2, HALF // 2)
        if d == 0:
            src, dst = field.at[h, own, 0:2, high, :], field.at[h, own, 2:4, low, :]
        elif d == 1:
            src, dst = field.at[h, own, 0:2, low, :], field.at[h, own, 2:4, high, :]
        elif d == 2:
            src, dst = field.at[h, own, 1], field.at[h, own, 4]
        elif d == 3:
            src, dst = field.at[h, own, 0], field.at[h, own, 5]
        elif d == 4:
            src, dst = z_out.at[h, c, 1], z_in.at[h, c, 0]
        else:
            src, dst = z_out.at[h, c, 0], z_in.at[h, c, 1]
        return pltpu.make_async_remote_copy(
            src_ref=src,
            dst_ref=dst,
            send_sem=halo_send.at[h, c, d],
            recv_sem=halo_recv.at[h, c, d],
            device_id=toward(d),
            device_id_type=pl.DeviceIdType.MESH,
        )

    def table(h, g, kind, d):
        return pltpu.make_async_remote_copy(
            src_ref=(table_out, scaled_out)[kind].at[h, g],
            dst_ref=(table_in, scaled_in)[kind].at[h, g, d],
            send_sem=table_send.at[h, g, kind, d],
            recv_sem=table_recv.at[h, g, kind, d],
            device_id=toward(d),
            device_id_type=pl.DeviceIdType.MESH,
        )

    def exchange(c):
        return pltpu.make_async_remote_copy(
            src_ref=filtered.at[pl.ds(c * CHUNK, CHUNK)],
            dst_ref=partner.at[pl.ds(c * CHUNK, CHUNK)],
            send_sem=band_send.at[c],
            recv_sem=band_recv.at[c],
            device_id={"band": 1 - band},
            device_id_type=pl.DeviceIdType.MESH,
        )

    def start_all(make):
        for d in range(6):

            @pl.when(has[d])
            def _():
                make(d).start()

    def wait_recv_all(make):
        for d in range(6):

            @pl.when(has[OPPOSITE[d]])
            def _():
                make(d).wait_recv()

    def wait_send_all(make):
        for d in range(6):

            @pl.when(has[d])
            def _():
                make(d).wait_send()

    def high_of(h, o):
        return field[h, o, 0:2].reshape(ROWS, CZ)

    def low_of(h, o):
        return field[h, o, 6:8].reshape(ROWS, CZ)

    def keep(h, o, values):
        high, low = split(values.reshape(2, HALF, CZ))
        field[h, o, 0:2] = high
        field[h, o, 6:8] = low

    def send_halos(h, c):
        ends = None
        for o in range(c * CHUNK, (c + 1) * CHUNK):
            part = dot(high_of(h, o), pack[o])
            ends = part if ends is None else ends + part
        z_out[h, c, 0] = ends[:, :CZ].astype(BF16)
        z_out[h, c, 1] = ends[:, CZ:].astype(BF16)
        start_all(lambda d: halo(h, c, d))

    for c in range(NCHUNK):
        for copy in orb_loads[c]:
            copy.wait()
        for o in range(c * CHUNK, (c + 1) * CHUNK):
            keep(0, o, start[o].reshape(ROWS, CZ))
        if c == 0:
            pack_load.wait()
            pl.semaphore_wait(barrier, partners)
        send_halos(0, c)

    proj_load.wait()
    mask = iota((32, CZ), 0) == iota((32, CZ), 1) // 4
    block = block_ref[...]
    row = ((block % 16) // 8) * HALF + (block // 16) * 8 + block % 8
    one_hot = (iota((ROWS, ENT), 0) == row).astype(F32).astype(BF16)
    spread[:, :ENT] = one_hot
    spread[:, ENT:] = one_hot
    diagonal = iota((ENT, ENT), 0) == iota((ENT, ENT), 1)
    row_column = jnp.sum(jnp.where(diagonal, row.astype(F32), 0.0), axis=1, keepdims=True)
    pick[...] = (iota((ENT, ROWS), 1).astype(F32) == row_column).astype(F32).astype(BF16)
    atom = atom_ref[...]
    gap = atom // OWNED - dom
    slot = jnp.zeros_like(gap)
    for d in range(6):
        slot = jnp.where(gap == strides[d], d + 1, slot)
    code = (slot * OWNED + atom % OWNED).astype(F32)
    code_column = jnp.sum(jnp.where(diagonal, code, 0.0), axis=1, keepdims=True)
    for q in range(8):
        lanes = jnp.sum(jnp.where(mask, code_column[q * 32 : (q + 1) * 32], 0.0), axis=0, keepdims=True)
        wanted = lanes * 4.0 + (iota((1, CZ), 1) % 4).astype(F32)
        slots[:, q * CZ : (q + 1) * CZ] = (iota((CZ, CZ), 0).astype(F32) == wanted).astype(F32).astype(BF16)

    energy_load.wait()
    here = dom * OWNED % width + iota((width, CZ), 1) // 4
    chosen = jnp.logical_and(iota((width, CZ), 0) == here, iota((width, CZ), 1) < 4 * OWNED)
    chosen = chosen.astype(F32).astype(BF16)
    high, low = split(energy[...])
    levels = dot(high, chosen) + dot(low, chosen)
    levels = jnp.where(iota((4, CZ), 1) % 4 == iota((4, CZ), 0), levels, 0.0)
    own_energy = jnp.sum(levels, axis=0, keepdims=True) * (SCALE / KINETIC)

    def project(h, g):
        for i in range(GROUP):
            o = g * GROUP + i
            both = jnp.concatenate([high_of(h, o), low_of(h, o)], axis=1)
            picked[:, i] = dot(pick[...], both).astype(BF16).reshape(8, 32, 2 * CZ)
        for q in range(8):
            values = proj[q * CZ : (q + 1) * CZ, :]
            pairs = dot(picked[q].reshape(GROUP * 32, 2 * CZ), jnp.concatenate([values, values], axis=1), NT)
            kept = jnp.where(mask.reshape(1, 4, 8, CZ), pairs.reshape(GROUP, 4, 8, CZ), 0.0)
            inner[:, q * CZ : (q + 1) * CZ] = jnp.sum(kept, axis=1).reshape(GROUP * 8, CZ)
        high, low = split(inner[...])
        sums = dot(jnp.concatenate([high, low], axis=0), slots[...], NT).reshape(2, GROUP, 8, CZ)
        table_out[h, g, 0:GROUP] = jnp.sum(jnp.sum(sums, axis=0), axis=1)
        start_all(lambda d: table(h, g, 0, d))

    def scale_sums(h, g):
        wait_recv_all(lambda d: table(h, g, 0, d))
        total = table_out[h, g]
        for d in range(6):
            total = total + pltpu.roll(table_in[h, g, d], CZ - LANE_SLOT * (d + 1), 1)
        scaled_out[h, g] = jnp.where(iota((8, CZ), 1) < LANE_SLOT, total * own_energy, 0.0)
        start_all(lambda d: table(h, g, 1, d))

    def add_projectors(h, g):
        wait_recv_all(lambda d: table(h, g, 1, d))
        scaled = scaled_out[h, g]
        for d in range(6):
            scaled = scaled + pltpu.roll(scaled_in[h, g, d], LANE_SLOT * (OPPOSITE[d] + 1), 1)
        high, low = split(scaled)
        entries = dot(jnp.concatenate([high, low], axis=0), slots[...])
        for q in range(8):
            lanes = slice(q * CZ, (q + 1) * CZ)
            rows = []
            for i in range(GROUP):
                rows.append(
                    jnp.concatenate(
                        [
                            jnp.where(mask, entries[i : i + 1, lanes], 0.0).astype(BF16),
                            jnp.where(mask, entries[8 + i : 9 + i, lanes], 0.0).astype(BF16),
                        ],
                        axis=1,
                    )
                )
            values = proj[lanes, :]
            added = dot(jnp.concatenate(rows, axis=0), jnp.concatenate([values, values], axis=0))
            high, low = split(added.reshape(GROUP, 32, CZ))
            additions[g * GROUP : (g + 1) * GROUP, 0, q * 32 : (q + 1) * 32] = high
            additions[g * GROUP : (g + 1) * GROUP, 1, q * 32 : (q + 1) * 32] = low

    def applied(h, c, o):
        total = dot(plane[...], field[h, o].reshape(8 * HALF, CZ))
        total = total + dot(jnp.concatenate([high_of(h, o), low_of(h, o)], axis=1), line[...])
        total = total + dot(jnp.concatenate([z_in[h, c, 0], z_in[h, c, 1]], axis=1), edge[o])
        return total + dot(spread[...], additions[o].reshape(2 * ENT, CZ))

    for g in range(NGROUP):
        project(0, g)

    jj = iota((CZ, 16), 0) // 16 + band * NORB
    choose_out = (iota((CZ, 16), 1) == jj).astype(F32).astype(BF16)
    column = iota((16, 2 * CZ), 1) // 16
    own = column < NORB
    wanted = jnp.where(own, column + band * NORB, column - NORB + (1 - band) * NORB)
    choose_in = (iota((16, 2 * CZ), 0) == wanted).astype(F32).astype(BF16)
    rows_of = dot(choose_out, panel_ref[...], NT).astype(BF16)
    spread_panel = dot(rows_of, choose_in)
    same = iota((CZ, 2 * CZ), 0) % 16 == iota((CZ, 2 * CZ), 1) % 16
    mix[...] = jnp.where(same, spread_panel, 0.0).astype(BF16)

    for copy in pot_loads:
        copy.wait()
    center = KINETIC * 3.0 * COEFFS[0] - CENTER
    weight[...] = (weight[...] + center) * (1.0 / HALF_WIDTH)
    slope = KINETIC / (SCALE * HALF_WIDTH)

    for g in range(NGROUP):
        scale_sums(0, g)
    for g in range(NGROUP):
        add_projectors(0, g)
    plane_load.wait()
    line_load.wait()
    edge_load.wait()

    def first_chunk(c):
        wait_recv_all(lambda d: halo(0, c, d))
        for o in range(c * CHUNK, (c + 1) * CHUNK):
            base = weight[...].reshape(ROWS, CZ) * start[o].reshape(ROWS, CZ)
            values = slope * applied(0, c, o) + base
            first[o] = values
            keep(1, o, values)
        send_halos(1, c)

    def second_chunk(c):
        wait_recv_all(lambda d: halo(1, c, d))
        for o in range(c * CHUNK, (c + 1) * CHUNK):
            base = weight[...].reshape(ROWS, CZ) * first[o]
            values = 2.0 * (slope * applied(1, c, o) + base) - start[o].reshape(ROWS, CZ)
            filtered[o] = values.astype(BF16).reshape(2, HALF, CZ)
        exchange(c).start()

    first_chunk(0)
    first_chunk(1)
    project(1, 0)
    first_chunk(2)
    first_chunk(3)
    project(1, 1)
    scale_sums(1, 0)
    add_projectors(1, 0)
    second_chunk(0)
    scale_sums(1, 1)
    second_chunk(1)
    add_projectors(1, 1)
    second_chunk(2)
    second_chunk(3)

    for c in range(NCHUNK):
        exchange(c).wait_recv()
    outs = []
    for h in range(2):
        for part in range(6):
            rows = slice(part * 16, (part + 1) * 16)
            cells = jnp.concatenate(
                [filtered[:, h, rows].reshape(CZ, CZ), partner[:, h, rows].reshape(CZ, CZ)], axis=0
            )
            result[:, h, 2 * part : 2 * part + 2] = dot(mix[...], cells).reshape(NORB, 2, 8, CZ)
        copy = pltpu.make_async_copy(result.at[:, h], out_hbm.at[0, :, :, pl.ds(h * 8, 8), :], out_sem.at[h])
        copy.start()
        outs.append(copy)

    for c in range(NCHUNK):
        exchange(c).wait_send()
    for h in range(2):
        for c in range(NCHUNK):
            wait_send_all(lambda d: halo(h, c, d))
        for g in range(NGROUP):
            for kind in range(2):
                wait_send_all(lambda d: table(h, g, kind, d))
    for copy in outs:
        copy.wait()


def shards(orbitals, potential, projectors, entry_atom, entry_block, kb_energy, panel):
    tables = [jnp.asarray(t) for t in stencil_tables()]
    anywhere = pl.BlockSpec(memory_space=pltpu.HBM)
    vmem = pl.BlockSpec(memory_space=pltpu.VMEM)
    dma = pltpu.SemaphoreType.DMA
    return pl.pallas_call(
        kernel,
        out_shape=jax.ShapeDtypeStruct((1, NORB, CX, CY, CZ), F32),
        in_specs=[anywhere, anywhere, anywhere, vmem, vmem, anywhere, vmem] + [anywhere] * 4,
        out_specs=anywhere,
        scratch_shapes=[
            pltpu.VMEM((NORB, 2, CX, 8, CZ), F32),
            pltpu.VMEM((2, NORB, 8, HALF, CZ), BF16),
            pltpu.VMEM((NORB, ROWS, CZ), F32),
            pltpu.VMEM((2, CX, 8, CZ), F32),
            pltpu.VMEM((4 * ENT, CZ), BF16),
            pltpu.VMEM((4, min(128, kb_energy.shape[0])), F32),
            pltpu.VMEM((ROWS, 8 * HALF), BF16),
            pltpu.VMEM((2 * CZ, CZ), BF16),
            pltpu.VMEM((NORB, 2 * CZ, CZ), BF16),
            pltpu.VMEM((NORB, CZ, 2 * CZ), BF16),
            pltpu.VMEM((2, NCHUNK, 2, ROWS, CZ), BF16),
            pltpu.VMEM((2, NCHUNK, 2, ROWS, CZ), BF16),
            pltpu.VMEM((NORB, 2, HALF, CZ), BF16),
            pltpu.VMEM((NORB, 2, HALF, CZ), BF16),
            pltpu.VMEM((NORB, 2, CX, 8, CZ), F32),
            pltpu.VMEM((ENT, ROWS), BF16),
            pltpu.VMEM((ROWS, 2 * ENT), BF16),
            pltpu.VMEM((CZ, 4 * ENT), BF16),
            pltpu.VMEM((8, GROUP, 32, 2 * CZ), BF16),
            pltpu.VMEM((GROUP * 8, 4 * ENT), F32),
            pltpu.VMEM((NORB, 2, ENT, CZ), BF16),
            pltpu.VMEM((2, NGROUP, 8, CZ), F32),
            pltpu.VMEM((2, NGROUP, 6, 8, CZ), F32),
            pltpu.VMEM((2, NGROUP, 8, CZ), F32),
            pltpu.VMEM((2, NGROUP, 6, 8, CZ), F32),
            pltpu.VMEM((CZ, 2 * CZ), BF16),
            dma((2 * NCHUNK + 8,)),
            dma((2, NCHUNK, 6)),
            dma((2, NCHUNK, 6)),
            dma((2, NGROUP, 2, 6)),
            dma((2, NGROUP, 2, 6)),
            dma((NCHUNK,)),
            dma((NCHUNK,)),
            dma((2,)),
        ],
        compiler_params=pltpu.CompilerParams(
            collective_id=0, has_side_effects=True, vmem_limit_bytes=62 * 1024 * 1024
        ),
    )(
        orbitals,
        potential,
        projectors.reshape(-1, projectors.shape[2]),
        entry_atom.reshape(1, -1),
        entry_block.reshape(1, -1),
        kb_energy.T,
        panel,
        *tables,
    )


def solution(mesh):
    in_specs = (
        P("dom", "band", None, None, None),
        P("dom", None, None, None),
        P("dom", None, None),
        P("dom"),
        P("dom"),
        P(),
        P(),
    )
    out_specs = P("dom", "band", None, None, None)
    return jax.shard_map(shards, mesh=mesh, in_specs=in_specs, out_specs=out_specs, check_vma=False)
```

```python
import jax
import jax.numpy as jnp
import ml_dtypes
import numpy as np
from jax import lax
from jax.experimental import pallas as pl
from jax.experimental.pallas import tpu as pltpu
from jax.sharding import PartitionSpec as P

COEFFS = (
    -5369.0 / 1800.0,
    12.0 / 7.0,
    -15.0 / 56.0,
    10.0 / 189.0,
    -1.0 / 112.0,
    2.0 / 1925.0,
    -1.0 / 16632.0,
)
KINETIC = -3.125
CENTER = 36.0
HALF_WIDTH = 34.0
REACH = 6

DOM_Z = 4
DOM_Y = 8
NORB = 8
CX, CY, CZ = 12, 16, 128
ENT = 256
ROWS = CX * CY
HALF = ROWS // 2
OWNED = 4
CHUNK = 2
NCHUNK = NORB // CHUNK
GROUP = 4
NGROUP = NORB // GROUP
LANE_SLOT = 16
SCALE = 64 * 1.0937445
F32 = jnp.float32
BF16 = jnp.bfloat16
OPPOSITE = (1, 0, 3, 2, 5, 4)
NN = (((1,), (0,)), ((), ()))
NT = (((1,), (1,)), ((), ()))


def tap(distance):
    return SCALE * COEFFS[abs(distance)]


def stencil_tables():
    plane = np.zeros((ROWS, 8 * HALF), np.float32)
    for x in range(CX):
        for y in range(CY):
            row = y // 8 * HALF + x * 8 + y % 8
            for step in (s for s in range(-REACH, REACH + 1) if s):
                to = x + step
                if 0 <= to < CX:
                    near = y // 8 * HALF + to * 8 + y % 8
                    plane[row, near] += tap(step)
                    plane[row, 6 * HALF + near] += tap(step)
                else:
                    place = (to + REACH) * 8 if to < 0 else HALF // 2 + (to - CX) * 8
                    plane[row, (2 + y // 8) * HALF + place + y % 8] += tap(step)
                to = y + step
                if 0 <= to < CY:
                    near = to // 8 * HALF + x * 8 + to % 8
                    plane[row, near] += tap(step)
                    plane[row, 6 * HALF + near] += tap(step)
                elif to < 0:
                    plane[row, 4 * HALF + x * 8 + to + 8] += tap(step)
                else:
                    plane[row, 5 * HALF + x * 8 + to - CY] += tap(step)
    line = np.zeros((2 * CZ, CZ), np.float32)
    edge = np.zeros((NORB, 2 * CZ, CZ), np.float32)
    pack = np.zeros((NORB, CZ, 2 * CZ), np.float32)
    for z in range(CZ):
        for step in (s for s in range(-REACH, REACH + 1) if s):
            to = z + step
            for o in range(NORB):
                if to < 0:
                    edge[o, o * LANE_SLOT + to + REACH, z] = tap(step)
                elif to >= CZ:
                    edge[o, CZ + o * LANE_SLOT + to - CZ, z] = tap(step)
            if 0 <= to < CZ:
                line[to, z] = line[CZ + to, z] = tap(step)
    for o in range(NORB):
        for k in range(REACH):
            pack[o, k, o * LANE_SLOT + k] = 1.0
            pack[o, CZ - REACH + k, CZ + o * LANE_SLOT + k] = 1.0
    return [t.astype(ml_dtypes.bfloat16) for t in (plane, line, edge, pack)]


def dot(a, b, dims=NN):
    return lax.dot_general(a, b, dims, preferred_element_type=F32)


def iota(shape, axis):
    return lax.broadcasted_iota(jnp.int32, shape, axis)


def split(values):
    high = values.astype(BF16)
    return high, (values - high.astype(F32)).astype(BF16)


def kernel(
    orb_hbm, pot_hbm, proj_hbm, atom_ref, block_ref, energy_hbm, panel_ref, plane_hbm, line_hbm, edge_hbm, pack_hbm,
    out_hbm,
    start, field, first, weight, proj, energy, plane, line, edge, pack,
    z_out, z_in, filtered, partner, result,
    pick, spread, slots, picked, inner, additions, table_out, table_in, scaled_out, scaled_in, mix,
    local_sem, halo_send, halo_recv, table_send, table_recv, band_send, band_recv, out_sem,
):
    dom = lax.axis_index("dom")
    band = lax.axis_index("band")
    count = lax.axis_size("dom")
    plane_size = DOM_Y * DOM_Z
    at = (dom // plane_size, dom // DOM_Z % DOM_Y, dom % DOM_Z)
    extents = (count // plane_size, DOM_Y, DOM_Z)
    strides = (plane_size, -plane_size, DOM_Z, -DOM_Z, 1, -1)
    has = []
    for axis in range(3):
        has.append(at[axis] < extents[axis] - 1)
        has.append(at[axis] > 0)

    def toward(d):
        return {"dom": jnp.clip(dom + strides[d], 0, count - 1)}

    loads = []

    def load(src, dst):
        copy = pltpu.make_async_copy(src, dst, local_sem.at[len(loads)])
        copy.start()
        loads.append(copy)
        return copy

    orb_loads = [
        [
            load(
                orb_hbm.at[0, pl.ds(c * CHUNK, CHUNK), :, pl.ds(h * 8, 8), :],
                start.at[pl.ds(c * CHUNK, CHUNK), h],
            )
            for h in range(2)
        ]
        for c in range(NCHUNK)
    ]
    pack_load = load(pack_hbm, pack)
    proj_load = load(proj_hbm, proj)
    pot_loads = [load(pot_hbm.at[0, :, pl.ds(h * 8, 8), :], weight.at[h]) for h in range(2)]
    width = energy.shape[1]
    energy_load = load(energy_hbm.at[:, pl.ds(pl.multiple_of(dom * OWNED // width * width, width), width)], energy)
    plane_load = load(plane_hbm, plane)
    line_load = load(line_hbm, line)
    edge_load = load(edge_hbm, edge)

    barrier = pltpu.get_barrier_semaphore()
    partners = jnp.int32(1)
    for d in range(6):
        partners = partners + has[d].astype(jnp.int32)

        @pl.when(has[d])
        def _():
            pl.semaphore_signal(barrier, inc=1, device_id=toward(d), device_id_type=pl.DeviceIdType.MESH)

    pl.semaphore_signal(barrier, inc=1, device_id={"band": 1 - band}, device_id_type=pl.DeviceIdType.MESH)

    for h in range(2):
        for d in range(6):

            @pl.when(jnp.logical_not(has[OPPOSITE[d]]))
            def _():
                if d == 0:
                    field[h, :, 2:4, 0 : HALF // 2, :] = jnp.zeros((NORB, 2, HALF // 2, CZ), BF16)
                elif d == 1:
                    field[h, :, 2:4, HALF // 2 : HALF, :] = jnp.zeros((NORB, 2, HALF // 2, CZ), BF16)
                elif d == 2:
                    field[h, :, 4, :, :] = jnp.zeros((NORB, HALF, CZ), BF16)
                elif d == 3:
                    field[h, :, 5, :, :] = jnp.zeros((NORB, HALF, CZ), BF16)
                else:
                    z_in[h, :, d - 4] = jnp.zeros((NCHUNK, ROWS, CZ), BF16)
                table_in[h, :, d] = jnp.zeros((NGROUP, 8, CZ), F32)
                scaled_in[h, :, d] = jnp.zeros((NGROUP, 8, CZ), F32)

    table_out[...] = jnp.zeros(table_out.shape, F32)

    def halo(h, c, d):
        own = pl.ds(c * CHUNK, CHUNK)
        low, high = pl.ds(0, HALF // 2), pl.ds(HALF // 2, HALF // 2)
        if d == 0:
            src, dst = field.at[h, own, 0:2, high, :], field.at[h, own, 2:4, low, :]
        elif d == 1:
            src, dst = field.at[h, own, 0:2, low, :], field.at[h, own, 2:4, high, :]
        elif d == 2:
            src, dst = field.at[h, own, 1], field.at[h, own, 4]
        elif d == 3:
            src, dst = field.at[h, own, 0], field.at[h, own, 5]
        elif d == 4:
            src, dst = z_out.at[h, c, 1], z_in.at[h, c, 0]
        else:
            src, dst = z_out.at[h, c, 0], z_in.at[h, c, 1]
        return pltpu.make_async_remote_copy(
            src_ref=src,
            dst_ref=dst,
            send_sem=halo_send.at[h, c, d],
            recv_sem=halo_recv.at[h, c, d],
            device_id=toward(d),
            device_id_type=pl.DeviceIdType.MESH,
        )

    def table(h, g, kind, d):
        return pltpu.make_async_remote_copy(
            src_ref=(table_out, scaled_out)[kind].at[h, g],
            dst_ref=(table_in, scaled_in)[kind].at[h, g, d],
            send_sem=table_send.at[h, g, kind, d],
            recv_sem=table_recv.at[h, g, kind, d],
            device_id=toward(d),
            device_id_type=pl.DeviceIdType.MESH,
        )

    def exchange(c):
        return pltpu.make_async_remote_copy(
            src_ref=filtered.at[pl.ds(c * CHUNK, CHUNK)],
            dst_ref=partner.at[pl.ds(c * CHUNK, CHUNK)],
            send_sem=band_send.at[c],
            recv_sem=band_recv.at[c],
            device_id={"band": 1 - band},
            device_id_type=pl.DeviceIdType.MESH,
        )

    def start_all(make):
        for d in range(6):

            @pl.when(has[d])
            def _():
                make(d).start()

    def wait_recv_all(make):
        for d in range(6):

            @pl.when(has[OPPOSITE[d]])
            def _():
                make(d).wait_recv()

    def wait_send_all(make):
        for d in range(6):

            @pl.when(has[d])
            def _():
                make(d).wait_send()

    def high_of(h, o):
        return field[h, o, 0:2].reshape(ROWS, CZ)

    def low_of(h, o):
        return field[h, o, 6:8].reshape(ROWS, CZ)

    def keep(h, o, values):
        high, low = split(values.reshape(2, HALF, CZ))
        field[h, o, 0:2] = high
        field[h, o, 6:8] = low

    def send_halos(h, c):
        ends = None
        for o in range(c * CHUNK, (c + 1) * CHUNK):
            part = dot(high_of(h, o), pack[o])
            ends = part if ends is None else ends + part
        z_out[h, c, 0] = ends[:, :CZ].astype(BF16)
        z_out[h, c, 1] = ends[:, CZ:].astype(BF16)
        start_all(lambda d: halo(h, c, d))

    for c in range(NCHUNK):
        for copy in orb_loads[c]:
            copy.wait()
        for o in range(c * CHUNK, (c + 1) * CHUNK):
            keep(0, o, start[o].reshape(ROWS, CZ))
        if c == 0:
            pack_load.wait()
            pl.semaphore_wait(barrier, partners)
            send_halos(0, c)

    proj_load.wait()
    mask = iota((32, CZ), 0) == iota((32, CZ), 1) // 4
    block = block_ref[...]
    row = ((block % 16) // 8) * HALF + (block // 16) * 8 + block % 8
    one_hot = (iota((ROWS, ENT), 0) == row).astype(F32).astype(BF16)
    spread[:, :ENT] = one_hot
    spread[:, ENT:] = one_hot
    diagonal = iota((ENT, ENT), 0) == iota((ENT, ENT), 1)
    row_column = jnp.sum(jnp.where(diagonal, row.astype(F32), 0.0), axis=1, keepdims=True)
    pick[...] = (iota((ENT, ROWS), 1).astype(F32) == row_column).astype(F32).astype(BF16)
    atom = atom_ref[...]
    gap = atom // OWNED - dom
    slot = jnp.zeros_like(gap)
    for d in range(6):
        slot = jnp.where(gap == strides[d], d + 1, slot)
    code = (slot * OWNED + atom % OWNED).astype(F32)
    code_column = jnp.sum(jnp.where(diagonal, code, 0.0), axis=1, keepdims=True)
    for q in range(8):
        lanes = jnp.sum(jnp.where(mask, code_column[q * 32 : (q + 1) * 32], 0.0), axis=0, keepdims=True)
        wanted = lanes * 4.0 + (iota((1, CZ), 1) % 4).astype(F32)
        slots[:, q * CZ : (q + 1) * CZ] = (iota((CZ, CZ), 0).astype(F32) == wanted).astype(F32).astype(BF16)

    energy_load.wait()
    here = dom * OWNED % width + iota((width, CZ), 1) // 4
    chosen = jnp.logical_and(iota((width, CZ), 0) == here, iota((width, CZ), 1) < 4 * OWNED)
    chosen = chosen.astype(F32).astype(BF16)
    high, low = split(energy[...])
    levels = dot(high, chosen) + dot(low, chosen)
    levels = jnp.where(iota((4, CZ), 1) % 4 == iota((4, CZ), 0), levels, 0.0)
    own_energy = jnp.sum(levels, axis=0, keepdims=True) * (SCALE / KINETIC)

    def project(h, g):
        for i in range(GROUP):
            o = g * GROUP + i
            both = jnp.concatenate([high_of(h, o), low_of(h, o)], axis=1)
            picked[:, i] = dot(pick[...], both).astype(BF16).reshape(8, 32, 2 * CZ)
        for q in range(8):
            values = proj[q * CZ : (q + 1) * CZ, :]
            pairs = dot(picked[q].reshape(GROUP * 32, 2 * CZ), jnp.concatenate([values, values], axis=1), NT)
            kept = jnp.where(mask.reshape(1, 4, 8, CZ), pairs.reshape(GROUP, 4, 8, CZ), 0.0)
            inner[:, q * CZ : (q + 1) * CZ] = jnp.sum(kept, axis=1).reshape(GROUP * 8, CZ)
        high, low = split(inner[...])
        sums = dot(jnp.concatenate([high, low], axis=0), slots[...], NT).reshape(2, GROUP, 8, CZ)
        table_out[h, g, 0:GROUP] = jnp.sum(jnp.sum(sums, axis=0), axis=1)
        start_all(lambda d: table(h, g, 0, d))

    def scale_sums(h, g):
        wait_recv_all(lambda d: table(h, g, 0, d))
        total = table_out[h, g]
        for d in range(6):
            total = total + pltpu.roll(table_in[h, g, d], CZ - LANE_SLOT * (d + 1), 1)
        scaled_out[h, g] = jnp.where(iota((8, CZ), 1) < LANE_SLOT, total * own_energy, 0.0)
        start_all(lambda d: table(h, g, 1, d))

    def add_projectors(h, g):
        wait_recv_all(lambda d: table(h, g, 1, d))
        scaled = scaled_out[h, g]
        for d in range(6):
            scaled = scaled + pltpu.roll(scaled_in[h, g, d], LANE_SLOT * (OPPOSITE[d] + 1), 1)
        high, low = split(scaled)
        entries = dot(jnp.concatenate([high, low], axis=0), slots[...])
        for q in range(8):
            lanes = slice(q * CZ, (q + 1) * CZ)
            rows = []
            for i in range(GROUP):
                rows.append(
                    jnp.concatenate(
                        [
                            jnp.where(mask, entries[i : i + 1, lanes], 0.0).astype(BF16),
                            jnp.where(mask, entries[8 + i : 9 + i, lanes], 0.0).astype(BF16),
                        ],
                        axis=1,
                    )
                )
            values = proj[lanes, :]
            added = dot(jnp.concatenate(rows, axis=0), jnp.concatenate([values, values], axis=0))
            high, low = split(added.reshape(GROUP, 32, CZ))
            additions[g * GROUP : (g + 1) * GROUP, 0, q * 32 : (q + 1) * 32] = high
            additions[g * GROUP : (g + 1) * GROUP, 1, q * 32 : (q + 1) * 32] = low

    def applied(h, c, o):
        total = dot(plane[...], field[h, o].reshape(8 * HALF, CZ))
        total = total + dot(jnp.concatenate([high_of(h, o), low_of(h, o)], axis=1), line[...])
        total = total + dot(jnp.concatenate([z_in[h, c, 0], z_in[h, c, 1]], axis=1), edge[o])
        return total + dot(spread[...], additions[o].reshape(2 * ENT, CZ))

    for g in range(NGROUP):
        project(0, g)
    send_halos(0, 1)

    jj = iota((CZ, 16), 0) // 16 + band * NORB
    choose_out = (iota((CZ, 16), 1) == jj).astype(F32).astype(BF16)
    column = iota((16, 2 * CZ), 1) // 16
    own = column < NORB
    wanted = jnp.where(own, column + band * NORB, column - NORB + (1 - band) * NORB)
    choose_in = (iota((16, 2 * CZ), 0) == wanted).astype(F32).astype(BF16)
    rows_of = dot(choose_out, panel_ref[...], NT).astype(BF16)
    spread_panel = dot(rows_of, choose_in)
    same = iota((CZ, 2 * CZ), 0) % 16 == iota((CZ, 2 * CZ), 1) % 16
    mix[...] = jnp.where(same, spread_panel, 0.0).astype(BF16)

    for copy in pot_loads:
        copy.wait()
    center = KINETIC * 3.0 * COEFFS[0] - CENTER
    weight[...] = (weight[...] + center) * (1.0 / HALF_WIDTH)
    slope = KINETIC / (SCALE * HALF_WIDTH)

    for g in range(NGROUP):
        scale_sums(0, g)
    send_halos(0, 2)
    send_halos(0, 3)
    for g in range(NGROUP):
        add_projectors(0, g)
    plane_load.wait()
    line_load.wait()
    edge_load.wait()

    def first_chunk(c):
        wait_recv_all(lambda d: halo(0, c, d))
        for o in range(c * CHUNK, (c + 1) * CHUNK):
            base = weight[...].reshape(ROWS, CZ) * start[o].reshape(ROWS, CZ)
            values = slope * applied(0, c, o) + base
            first[o] = values
            keep(1, o, values)

    def second_chunk(c):
        wait_recv_all(lambda d: halo(1, c, d))
        for o in range(c * CHUNK, (c + 1) * CHUNK):
            base = weight[...].reshape(ROWS, CZ) * first[o]
            values = 2.0 * (slope * applied(1, c, o) + base) - start[o].reshape(ROWS, CZ)
            filtered[o] = values.astype(BF16).reshape(2, HALF, CZ)
        exchange(c).start()

    first_chunk(0)
    send_halos(1, 0)
    first_chunk(1)
    project(1, 0)
    send_halos(1, 1)
    first_chunk(2)
    first_chunk(3)
    project(1, 1)
    scale_sums(1, 0)
    send_halos(1, 2)
    scale_sums(1, 1)
    send_halos(1, 3)
    add_projectors(1, 0)
    second_chunk(0)
    second_chunk(1)
    add_projectors(1, 1)
    second_chunk(2)
    second_chunk(3)

    for c in range(NCHUNK):
        exchange(c).wait_recv()
    outs = []
    for h in range(2):
        for part in range(6):
            rows = slice(part * 16, (part + 1) * 16)
            cells = jnp.concatenate(
                [filtered[:, h, rows].reshape(CZ, CZ), partner[:, h, rows].reshape(CZ, CZ)], axis=0
            )
            result[:, h, 2 * part : 2 * part + 2] = dot(mix[...], cells).reshape(NORB, 2, 8, CZ)
        copy = pltpu.make_async_copy(result.at[:, h], out_hbm.at[0, :, :, pl.ds(h * 8, 8), :], out_sem.at[h])
        copy.start()
        outs.append(copy)

    for c in range(NCHUNK):
        exchange(c).wait_send()
    for h in range(2):
        for c in range(NCHUNK):
            wait_send_all(lambda d: halo(h, c, d))
        for g in range(NGROUP):
            for kind in range(2):
                wait_send_all(lambda d: table(h, g, kind, d))
    for copy in outs:
        copy.wait()


def shards(orbitals, potential, projectors, entry_atom, entry_block, kb_energy, panel):
    tables = [jnp.asarray(t) for t in stencil_tables()]
    anywhere = pl.BlockSpec(memory_space=pltpu.HBM)
    vmem = pl.BlockSpec(memory_space=pltpu.VMEM)
    dma = pltpu.SemaphoreType.DMA
    return pl.pallas_call(
        kernel,
        out_shape=jax.ShapeDtypeStruct((1, NORB, CX, CY, CZ), F32),
        in_specs=[anywhere, anywhere, anywhere, vmem, vmem, anywhere, vmem] + [anywhere] * 4,
        out_specs=anywhere,
        scratch_shapes=[
            pltpu.VMEM((NORB, 2, CX, 8, CZ), F32),
            pltpu.VMEM((2, NORB, 8, HALF, CZ), BF16),
            pltpu.VMEM((NORB, ROWS, CZ), F32),
            pltpu.VMEM((2, CX, 8, CZ), F32),
            pltpu.VMEM((4 * ENT, CZ), BF16),
            pltpu.VMEM((4, min(128, kb_energy.shape[0])), F32),
            pltpu.VMEM((ROWS, 8 * HALF), BF16),
            pltpu.VMEM((2 * CZ, CZ), BF16),
            pltpu.VMEM((NORB, 2 * CZ, CZ), BF16),
            pltpu.VMEM((NORB, CZ, 2 * CZ), BF16),
            pltpu.VMEM((2, NCHUNK, 2, ROWS, CZ), BF16),
            pltpu.VMEM((2, NCHUNK, 2, ROWS, CZ), BF16),
            pltpu.VMEM((NORB, 2, HALF, CZ), BF16),
            pltpu.VMEM((NORB, 2, HALF, CZ), BF16),
            pltpu.VMEM((NORB, 2, CX, 8, CZ), F32),
            pltpu.VMEM((ENT, ROWS), BF16),
            pltpu.VMEM((ROWS, 2 * ENT), BF16),
            pltpu.VMEM((CZ, 4 * ENT), BF16),
            pltpu.VMEM((8, GROUP, 32, 2 * CZ), BF16),
            pltpu.VMEM((GROUP * 8, 4 * ENT), F32),
            pltpu.VMEM((NORB, 2, ENT, CZ), BF16),
            pltpu.VMEM((2, NGROUP, 8, CZ), F32),
            pltpu.VMEM((2, NGROUP, 6, 8, CZ), F32),
            pltpu.VMEM((2, NGROUP, 8, CZ), F32),
            pltpu.VMEM((2, NGROUP, 6, 8, CZ), F32),
            pltpu.VMEM((CZ, 2 * CZ), BF16),
            dma((2 * NCHUNK + 8,)),
            dma((2, NCHUNK, 6)),
            dma((2, NCHUNK, 6)),
            dma((2, NGROUP, 2, 6)),
            dma((2, NGROUP, 2, 6)),
            dma((NCHUNK,)),
            dma((NCHUNK,)),
            dma((2,)),
        ],
        compiler_params=pltpu.CompilerParams(
            collective_id=0, has_side_effects=True, vmem_limit_bytes=62 * 1024 * 1024
        ),
    )(
        orbitals,
        potential,
        projectors.reshape(-1, projectors.shape[2]),
        entry_atom.reshape(1, -1),
        entry_block.reshape(1, -1),
        kb_energy.T,
        panel,
        *tables,
    )


def solution(mesh):
    in_specs = (
        P("dom", "band", None, None, None),
        P("dom", None, None, None),
        P("dom", None, None),
        P("dom"),
        P("dom"),
        P(),
        P(),
    )
    out_specs = P("dom", "band", None, None, None)
    return jax.shard_map(shards, mesh=mesh, in_specs=in_specs, out_specs=out_specs, check_vma=False)
```

```python
import jax
import jax.numpy as jnp
import ml_dtypes
import numpy as np
from jax import lax
from jax.experimental import pallas as pl
from jax.experimental.pallas import tpu as pltpu
from jax.sharding import PartitionSpec as P

COEFFS = (
    -5369.0 / 1800.0,
    12.0 / 7.0,
    -15.0 / 56.0,
    10.0 / 189.0,
    -1.0 / 112.0,
    2.0 / 1925.0,
    -1.0 / 16632.0,
)
KINETIC = -3.125
CENTER = 36.0
HALF_WIDTH = 34.0
REACH = 6

DOM_Z = 4
DOM_Y = 8
NORB = 8
CX, CY, CZ = 12, 16, 128
ENT = 256
ROWS = CX * CY
HALF = ROWS // 2
OWNED = 4
CHUNK = 2
NCHUNK = NORB // CHUNK
GROUP = 4
NGROUP = NORB // GROUP
MID_Y = DOM_Y // 2
RELAYED = (0, 1) if MID_Y > 1 else ()
LANE_SLOT = 16
XPARTS = 1
SCALE = 64 * 1.0937445
F32 = jnp.float32
BF16 = jnp.bfloat16
OPPOSITE = (1, 0, 3, 2, 5, 4)
NN = (((1,), (0,)), ((), ()))
NT = (((1,), (1,)), ((), ()))


def tap(distance):
    return SCALE * COEFFS[abs(distance)]


def stencil_tables():
    plane = np.zeros((ROWS, 8 * HALF), np.float32)
    for x in range(CX):
        for y in range(CY):
            row = y // 8 * HALF + x * 8 + y % 8
            for step in (s for s in range(-REACH, REACH + 1) if s):
                to = x + step
                if 0 <= to < CX:
                    near = y // 8 * HALF + to * 8 + y % 8
                    plane[row, near] += tap(step)
                    plane[row, 6 * HALF + near] += tap(step)
                else:
                    place = (to + REACH) * 8 if to < 0 else HALF // 2 + (to - CX) * 8
                    plane[row, (2 + y // 8) * HALF + place + y % 8] += tap(step)
                to = y + step
                if 0 <= to < CY:
                    near = to // 8 * HALF + x * 8 + to % 8
                    plane[row, near] += tap(step)
                    plane[row, 6 * HALF + near] += tap(step)
                elif to < 0:
                    plane[row, 4 * HALF + x * 8 + to + 8] += tap(step)
                else:
                    plane[row, 5 * HALF + x * 8 + to - CY] += tap(step)
    line = np.zeros((2 * CZ, CZ), np.float32)
    edge = np.zeros((NORB, 2 * CZ, CZ), np.float32)
    pack = np.zeros((NORB, CZ, 2 * CZ), np.float32)
    for z in range(CZ):
        for step in (s for s in range(-REACH, REACH + 1) if s):
            to = z + step
            for o in range(NORB):
                if to < 0:
                    edge[o, o * LANE_SLOT + to + REACH, z] = tap(step)
                elif to >= CZ:
                    edge[o, CZ + o * LANE_SLOT + to - CZ, z] = tap(step)
            if 0 <= to < CZ:
                line[to, z] = line[CZ + to, z] = tap(step)
    for o in range(NORB):
        for k in range(REACH):
            pack[o, k, o * LANE_SLOT + k] = 1.0
            pack[o, CZ - REACH + k, CZ + o * LANE_SLOT + k] = 1.0
    return [t.astype(ml_dtypes.bfloat16) for t in (plane, line, edge, pack)]


def dot(a, b, dims=NN):
    return lax.dot_general(a, b, dims, preferred_element_type=F32)


def iota(shape, axis):
    return lax.broadcasted_iota(jnp.int32, shape, axis)


def split(values):
    high = values.astype(BF16)
    return high, (values - high.astype(F32)).astype(BF16)


def kernel(
    orb_hbm, pot_hbm, proj_hbm, atom_ref, block_ref, energy_hbm, panel_ref, plane_hbm, line_hbm, edge_hbm, pack_hbm,
    own_hbm, partner_hbm, mix_hbm,
    start, field, first, weight, proj, energy, plane, line, edge, pack,
    z_out, z_in, filtered,
    pick, spread, slots, picked, inner, additions, table_out, table_in, scaled_out, scaled_in, mix, relay_in,
    local_sem, halo_send, halo_recv, table_send, table_recv, band_send, band_recv, relay_send, relay_recv, out_sem,
):
    dom = lax.axis_index("dom")
    band = lax.axis_index("band")
    count = lax.axis_size("dom")
    plane_size = DOM_Y * DOM_Z
    at = (dom // plane_size, dom // DOM_Z % DOM_Y, dom % DOM_Z)
    extents = (count // plane_size, DOM_Y, DOM_Z)
    strides = (plane_size, -plane_size, DOM_Z, -DOM_Z, 1, -1)
    has = []
    for axis in range(3):
        has.append(at[axis] < extents[axis] - 1)
        has.append(at[axis] > 0)

    def toward(d):
        return {"dom": jnp.clip(dom + strides[d], 0, count - 1)}

    def away(offset):
        return {"dom": jnp.clip(dom + offset * DOM_Z, 0, count - 1)}

    relay_pairs = (
        (0, (MID_Y - 1, MID_Y)),
        (MID_Y - 1, (1 - MID_Y, MID_Y)),
        (MID_Y, (MID_Y - 1, -MID_Y)),
        (DOM_Y - 1, (1 - MID_Y, -MID_Y)),
    )
    routes = {
        2: (MID_Y - 1, 1 - MID_Y, 0, MID_Y),
        3: (MID_Y, MID_Y - 1, DOM_Y - 1, -MID_Y),
    }

    barrier = pltpu.get_barrier_semaphore()
    partners = jnp.int32(1)
    for d in range(6):
        partners = partners + has[d].astype(jnp.int32)

        @pl.when(has[d])
        def _():
            pl.semaphore_signal(barrier, inc=1, device_id=toward(d), device_id_type=pl.DeviceIdType.MESH)

    pl.semaphore_signal(barrier, inc=1, device_id={"band": 1 - band}, device_id_type=pl.DeviceIdType.MESH)
    for place, offsets in relay_pairs if RELAYED else ():
        partners = partners + jnp.where(at[1] == place, 2, 0)

        @pl.when(at[1] == place)
        def _():
            for offset in offsets:
                pl.semaphore_signal(
                    barrier, inc=1, device_id=away(offset), device_id_type=pl.DeviceIdType.MESH
                )

    loads = []

    def load(src, dst):
        copy = pltpu.make_async_copy(src, dst, local_sem.at[len(loads)])
        copy.start()
        loads.append(copy)
        return copy

    orb_loads = [
        [
            load(
                orb_hbm.at[0, pl.ds(c * CHUNK, CHUNK), :, pl.ds(h * 8, 8), :],
                start.at[pl.ds(c * CHUNK, CHUNK), h],
            )
            for h in range(2)
        ]
        for c in range(NCHUNK)
    ]
    pack_load = load(pack_hbm, pack)
    proj_load = load(proj_hbm, proj)
    pot_loads = [load(pot_hbm.at[0, :, pl.ds(h * 8, 8), :], weight.at[h]) for h in range(2)]
    width = energy.shape[1]
    energy_load = load(energy_hbm.at[:, pl.ds(pl.multiple_of(dom * OWNED // width * width, width), width)], energy)
    plane_load = load(plane_hbm, plane)
    line_load = load(line_hbm, line)
    edge_load = load(edge_hbm, edge)

    for h in range(2):
        for d in range(6):

            @pl.when(jnp.logical_not(has[OPPOSITE[d]]))
            def _():
                if d == 0:
                    field[h, :, 2:4, 0 : HALF // 2, :] = jnp.zeros((NORB, 2, HALF // 2, CZ), BF16)
                elif d == 1:
                    field[h, :, 2:4, HALF // 2 : HALF, :] = jnp.zeros((NORB, 2, HALF // 2, CZ), BF16)
                elif d == 2:
                    field[h, :, 4, :, :] = jnp.zeros((NORB, HALF, CZ), BF16)
                elif d == 3:
                    field[h, :, 5, :, :] = jnp.zeros((NORB, HALF, CZ), BF16)
                else:
                    z_in[h, :, d - 4] = jnp.zeros((NCHUNK, ROWS, CZ), BF16)
                table_in[h, d] = jnp.zeros((NGROUP, 8, CZ), F32)
                scaled_in[h, d] = jnp.zeros((NGROUP, 8, CZ), F32)

    table_out[...] = jnp.zeros(table_out.shape, F32)

    def halo(h, c, d):
        own = pl.ds(c * CHUNK, CHUNK)
        low, high = pl.ds(0, HALF // 2), pl.ds(HALF // 2, HALF // 2)
        if d == 0:
            src, dst = field.at[h, own, 0:2, high, :], field.at[h, own, 2:4, low, :]
        elif d == 1:
            src, dst = field.at[h, own, 0:2, low, :], field.at[h, own, 2:4, high, :]
        elif d == 2:
            src, dst = field.at[h, own, 1], field.at[h, own, 4]
        elif d == 3:
            src, dst = field.at[h, own, 0], field.at[h, own, 5]
        elif d == 4:
            src, dst = z_out.at[h, c, 1], z_in.at[h, c, 0]
        else:
            src, dst = z_out.at[h, c, 0], z_in.at[h, c, 1]
        return pltpu.make_async_remote_copy(
            src_ref=src,
            dst_ref=dst,
            send_sem=halo_send.at[h, c, d],
            recv_sem=halo_recv.at[h, c, d],
            device_id=toward(d),
            device_id_type=pl.DeviceIdType.MESH,
        )

    def to_relay(h, c, d):
        return pltpu.make_async_remote_copy(
            src_ref=field.at[h, pl.ds(c * CHUNK, CHUNK), 3 - d],
            dst_ref=relay_in.at[h, RELAYED.index(c)],
            send_sem=halo_send.at[h, c, d],
            recv_sem=relay_recv.at[h, RELAYED.index(c)],
            device_id=away(routes[d][1]),
            device_id_type=pl.DeviceIdType.MESH,
        )

    def from_relay(h, c, d):
        return pltpu.make_async_remote_copy(
            src_ref=relay_in.at[h, RELAYED.index(c)],
            dst_ref=field.at[h, pl.ds(c * CHUNK, CHUNK), 2 + d],
            send_sem=relay_send.at[h, RELAYED.index(c)],
            recv_sem=halo_recv.at[h, c, d],
            device_id=away(routes[d][3]),
            device_id_type=pl.DeviceIdType.MESH,
        )

    def forward(h, c):
        for d in routes if c in RELAYED else ():

            @pl.when(at[1] == routes[d][2])
            def _():
                to_relay(h, c, d).wait_recv()
                from_relay(h, c, d).start()

    def table(h, gs, kind, d):
        return pltpu.make_async_remote_copy(
            src_ref=(table_out, scaled_out)[kind].at[h, pl.ds(gs[0], len(gs))],
            dst_ref=(table_in, scaled_in)[kind].at[h, d, pl.ds(gs[0], len(gs))],
            send_sem=table_send.at[h, gs[0], kind, d],
            recv_sem=table_recv.at[h, gs[0], kind, d],
            device_id=toward(d),
            device_id_type=pl.DeviceIdType.MESH,
        )

    def exchange(o):
        return pltpu.make_async_remote_copy(
            src_ref=filtered.at[o],
            dst_ref=partner_hbm.at[o],
            send_sem=band_send.at[o],
            recv_sem=band_recv.at[o],
            device_id={"band": 1 - band},
            device_id_type=pl.DeviceIdType.MESH,
        )

    def store(o):
        return pltpu.make_async_copy(filtered.at[o], own_hbm.at[o], out_sem.at[o])

    def start_all(make):
        for d in range(6):

            @pl.when(has[d])
            def _():
                make(d).start()

    def wait_recv_all(make):
        for d in range(6):

            @pl.when(has[OPPOSITE[d]])
            def _():
                make(d).wait_recv()

    def wait_send_all(make):
        for d in range(6):

            @pl.when(has[d])
            def _():
                make(d).wait_send()

    def high_of(h, o):
        return field[h, o, 0:2].reshape(ROWS, CZ)

    def low_of(h, o):
        return field[h, o, 6:8].reshape(ROWS, CZ)

    def keep(h, o, values):
        high, low = split(values.reshape(2, HALF, CZ))
        field[h, o, 0:2] = high
        field[h, o, 6:8] = low

    def send_halos(h, c):
        ends = None
        for o in range(c * CHUNK, (c + 1) * CHUNK):
            part = dot(high_of(h, o), pack[o])
            ends = part if ends is None else ends + part
        z_out[h, c, 0] = ends[:, :CZ].astype(BF16)
        z_out[h, c, 1] = ends[:, CZ:].astype(BF16)
        for d in range(6):
            direct = has[d]
            if d in routes and c in RELAYED:
                direct = jnp.logical_and(direct, at[1] != routes[d][0])

                @pl.when(at[1] == routes[d][0])
                def _():
                    to_relay(h, c, d).start()

            @pl.when(direct)
            def _():
                halo(h, c, d).start()

    for c in range(NCHUNK):
        for copy in orb_loads[c]:
            copy.wait()
        for o in range(c * CHUNK, (c + 1) * CHUNK):
            keep(0, o, start[o].reshape(ROWS, CZ))
        if c == 0:
            pack_load.wait()
            pl.semaphore_wait(barrier, partners)
            send_halos(0, c)

    every = tuple(range(NGROUP))

    proj_load.wait()
    mask = iota((32, CZ), 0) == iota((32, CZ), 1) // 4
    block = block_ref[...]
    row = ((block % 16) // 8) * HALF + (block // 16) * 8 + block % 8
    one_hot = (iota((ROWS, ENT), 0) == row).astype(F32).astype(BF16)
    spread[:, :ENT] = one_hot
    spread[:, ENT:] = one_hot
    diagonal = iota((ENT, ENT), 0) == iota((ENT, ENT), 1)
    row_column = jnp.sum(jnp.where(diagonal, row.astype(F32), 0.0), axis=1, keepdims=True)
    pick[...] = (iota((ENT, ROWS), 1).astype(F32) == row_column).astype(F32).astype(BF16)
    atom = atom_ref[...]
    gap = atom // OWNED - dom
    slot = jnp.zeros_like(gap)
    for d in range(6):
        slot = jnp.where(gap == strides[d], d + 1, slot)
    code = (slot * OWNED + atom % OWNED).astype(F32)
    code_column = jnp.sum(jnp.where(diagonal, code, 0.0), axis=1, keepdims=True)
    for q in range(8):
        lanes = jnp.sum(jnp.where(mask, code_column[q * 32 : (q + 1) * 32], 0.0), axis=0, keepdims=True)
        wanted = lanes * 4.0 + (iota((1, CZ), 1) % 4).astype(F32)
        slots[:, q * CZ : (q + 1) * CZ] = (iota((CZ, CZ), 0).astype(F32) == wanted).astype(F32).astype(BF16)

    energy_load.wait()
    here = dom * OWNED % width + iota((width, CZ), 1) // 4
    chosen = jnp.logical_and(iota((width, CZ), 0) == here, iota((width, CZ), 1) < 4 * OWNED)
    chosen = chosen.astype(F32).astype(BF16)
    high, low = split(energy[...])
    levels = dot(high, chosen) + dot(low, chosen)
    levels = jnp.where(iota((4, CZ), 1) % 4 == iota((4, CZ), 0), levels, 0.0)
    own_energy = jnp.sum(levels, axis=0, keepdims=True) * (SCALE / KINETIC)

    def project(h, g):
        for i in range(GROUP):
            o = g * GROUP + i
            both = jnp.concatenate([high_of(h, o), low_of(h, o)], axis=1)
            picked[:, i] = dot(pick[...], both).astype(BF16).reshape(8, 32, 2 * CZ)
        for q in range(8):
            values = proj[q * CZ : (q + 1) * CZ, :]
            pairs = dot(picked[q].reshape(GROUP * 32, 2 * CZ), jnp.concatenate([values, values], axis=1), NT)
            kept = jnp.where(mask.reshape(1, 4, 8, CZ), pairs.reshape(GROUP, 4, 8, CZ), 0.0)
            inner[:, q * CZ : (q + 1) * CZ] = jnp.sum(kept, axis=1).reshape(GROUP * 8, CZ)
        high, low = split(inner[...])
        sums = dot(jnp.concatenate([high, low], axis=0), slots[...], NT).reshape(2, GROUP, 8, CZ)
        table_out[h, g, 0:GROUP] = jnp.sum(jnp.sum(sums, axis=0), axis=1)

    def send_sums(h, gs):
        start_all(lambda d: table(h, gs, 0, d))

    def scale_sums(h, gs):
        wait_recv_all(lambda d: table(h, gs, 0, d))
        for g in gs:
            total = table_out[h, g]
            for d in range(6):
                total = total + pltpu.roll(table_in[h, d, g], CZ - LANE_SLOT * (d + 1), 1)
            scaled_out[h, g] = jnp.where(iota((8, CZ), 1) < LANE_SLOT, total * own_energy, 0.0)
        start_all(lambda d: table(h, gs, 1, d))

    def wait_scaled(h, gs):
        wait_recv_all(lambda d: table(h, gs, 1, d))

    def add_projectors(h, g):
        scaled = scaled_out[h, g]
        for d in range(6):
            scaled = scaled + pltpu.roll(scaled_in[h, d, g], LANE_SLOT * (OPPOSITE[d] + 1), 1)
        high, low = split(scaled)
        entries = dot(jnp.concatenate([high, low], axis=0), slots[...])
        for q in range(8):
            lanes = slice(q * CZ, (q + 1) * CZ)
            rows = []
            for i in range(GROUP):
                rows.append(
                    jnp.concatenate(
                        [
                            jnp.where(mask, entries[i : i + 1, lanes], 0.0).astype(BF16),
                            jnp.where(mask, entries[8 + i : 9 + i, lanes], 0.0).astype(BF16),
                        ],
                        axis=1,
                    )
                )
            values = proj[lanes, :]
            added = dot(jnp.concatenate(rows, axis=0), jnp.concatenate([values, values], axis=0))
            high, low = split(added.reshape(GROUP, 32, CZ))
            additions[g * GROUP : (g + 1) * GROUP, 0, q * 32 : (q + 1) * 32] = high
            additions[g * GROUP : (g + 1) * GROUP, 1, q * 32 : (q + 1) * 32] = low

    def applied(h, c, o):
        total = dot(plane[...], field[h, o].reshape(8 * HALF, CZ))
        total = total + dot(jnp.concatenate([high_of(h, o), low_of(h, o)], axis=1), line[...])
        total = total + dot(jnp.concatenate([z_in[h, c, 0], z_in[h, c, 1]], axis=1), edge[o])
        return total + dot(spread[...], additions[o].reshape(2 * ENT, CZ))

    for g in range(NGROUP):
        project(0, g)
    send_sums(0, every)
    send_halos(0, 1)
    send_halos(0, 2)

    jj = iota((CZ, 16), 0) // 16 + band * NORB
    choose_out = (iota((CZ, 16), 1) == jj).astype(F32).astype(BF16)
    column = iota((16, 2 * CZ), 1) // 16
    own = column < NORB
    wanted = jnp.where(own, column + band * NORB, column - NORB + (1 - band) * NORB)
    choose_in = (iota((16, 2 * CZ), 0) == wanted).astype(F32).astype(BF16)
    rows_of = dot(choose_out, panel_ref[...], NT).astype(BF16)
    spread_panel = dot(rows_of, choose_in)
    same = iota((CZ, 2 * CZ), 0) % 16 == iota((CZ, 2 * CZ), 1) % 16
    mix[...] = jnp.where(same, spread_panel, 0.0).astype(BF16)
    mix_store = pltpu.make_async_copy(mix, mix_hbm, out_sem.at[NORB])
    mix_store.start()

    for copy in pot_loads:
        copy.wait()
    center = KINETIC * 3.0 * COEFFS[0] - CENTER
    weight[...] = (weight[...] + center) * (1.0 / HALF_WIDTH)
    slope = KINETIC / (SCALE * HALF_WIDTH)

    scale_sums(0, every)
    forward(0, 0)
    send_halos(0, 3)
    forward(0, 1)
    wait_scaled(0, every)
    for g in every:
        add_projectors(0, g)
    plane_load.wait()
    line_load.wait()
    edge_load.wait()

    def first_chunk(c):
        wait_recv_all(lambda d: halo(0, c, d))
        for o in range(c * CHUNK, (c + 1) * CHUNK):
            base = weight[...].reshape(ROWS, CZ) * start[o].reshape(ROWS, CZ)
            values = slope * applied(0, c, o) + base
            first[o] = values
            keep(1, o, values)

    def second_chunk(c):
        wait_recv_all(lambda d: halo(1, c, d))
        for o in range(c * CHUNK, (c + 1) * CHUNK):
            base = weight[...].reshape(ROWS, CZ) * first[o]
            values = 2.0 * (slope * applied(1, c, o) + base) - start[o].reshape(ROWS, CZ)
            filtered[o] = values.astype(BF16).reshape(2, HALF, CZ)
            exchange(o).start()
            store(o).start()

    first_chunk(0)
    send_halos(1, 0)
    first_chunk(1)
    project(1, 0)
    send_sums(1, (0,))
    send_halos(1, 1)
    first_chunk(2)
    first_chunk(3)
    project(1, 1)
    send_sums(1, (1,))
    scale_sums(1, (0,))
    forward(1, 0)
    send_halos(1, 2)
    forward(1, 1)
    scale_sums(1, (1,))
    send_halos(1, 3)
    wait_scaled(1, (0,))
    add_projectors(1, 0)
    second_chunk(0)
    second_chunk(1)
    wait_scaled(1, (1,))
    add_projectors(1, 1)
    second_chunk(2)
    second_chunk(3)

    for o in range(NORB):
        exchange(o).wait_recv()
    for o in range(NORB):
        exchange(o).wait_send()
    for h in range(2):
        for c in range(NCHUNK):
            wait_send_all(lambda d: halo(h, c, d))
        for gs in (every,) if h == 0 else tuple((g,) for g in every):
            for kind in range(2):
                wait_send_all(lambda d: table(h, gs, kind, d))
        for c in RELAYED:
            for d in routes:

                @pl.when(at[1] == routes[d][2])
                def _():
                    from_relay(h, c, d).wait_send()
    for o in range(NORB):
        store(o).wait()
    mix_store.wait()


def rotate(own, partner, mix, out):
    for part in range(CX // XPARTS // 2):
        rows = slice(part * 16, (part + 1) * 16)
        cells = jnp.concatenate([own[:, 0, rows].reshape(CZ, CZ), partner[:, 0, rows].reshape(CZ, CZ)], axis=0)
        out[0, :, 2 * part : 2 * part + 2] = dot(mix[...], cells).reshape(NORB, 2, 8, CZ)


def shards(orbitals, potential, projectors, entry_atom, entry_block, kb_energy, panel):
    tables = [jnp.asarray(t) for t in stencil_tables()]
    anywhere = pl.BlockSpec(memory_space=pltpu.HBM)
    vmem = pl.BlockSpec(memory_space=pltpu.VMEM)
    dma = pltpu.SemaphoreType.DMA
    own, partner, mix = pl.pallas_call(
        kernel,
        out_shape=(
            jax.ShapeDtypeStruct((NORB, 2, HALF, CZ), BF16),
            jax.ShapeDtypeStruct((NORB, 2, HALF, CZ), BF16),
            jax.ShapeDtypeStruct((CZ, 2 * CZ), BF16),
        ),
        in_specs=[anywhere, anywhere, anywhere, vmem, vmem, anywhere, vmem] + [anywhere] * 4,
        out_specs=(anywhere,) * 3,
        scratch_shapes=[
            pltpu.VMEM((NORB, 2, CX, 8, CZ), F32),
            pltpu.VMEM((2, NORB, 8, HALF, CZ), BF16),
            pltpu.VMEM((NORB, ROWS, CZ), F32),
            pltpu.VMEM((2, CX, 8, CZ), F32),
            pltpu.VMEM((4 * ENT, CZ), BF16),
            pltpu.VMEM((4, min(128, kb_energy.shape[0])), F32),
            pltpu.VMEM((ROWS, 8 * HALF), BF16),
            pltpu.VMEM((2 * CZ, CZ), BF16),
            pltpu.VMEM((NORB, 2 * CZ, CZ), BF16),
            pltpu.VMEM((NORB, CZ, 2 * CZ), BF16),
            pltpu.VMEM((2, NCHUNK, 2, ROWS, CZ), BF16),
            pltpu.VMEM((2, NCHUNK, 2, ROWS, CZ), BF16),
            pltpu.VMEM((NORB, 2, HALF, CZ), BF16),
            pltpu.VMEM((ENT, ROWS), BF16),
            pltpu.VMEM((ROWS, 2 * ENT), BF16),
            pltpu.VMEM((CZ, 4 * ENT), BF16),
            pltpu.VMEM((8, GROUP, 32, 2 * CZ), BF16),
            pltpu.VMEM((GROUP * 8, 4 * ENT), F32),
            pltpu.VMEM((NORB, 2, ENT, CZ), BF16),
            pltpu.VMEM((2, NGROUP, 8, CZ), F32),
            pltpu.VMEM((2, 6, NGROUP, 8, CZ), F32),
            pltpu.VMEM((2, NGROUP, 8, CZ), F32),
            pltpu.VMEM((2, 6, NGROUP, 8, CZ), F32),
            pltpu.VMEM((CZ, 2 * CZ), BF16),
            pltpu.VMEM((2, max(1, len(RELAYED)), CHUNK, HALF, CZ), BF16),
            dma((2 * NCHUNK + 8,)),
            dma((2, NCHUNK, 6)),
            dma((2, NCHUNK, 6)),
            dma((2, NGROUP, 2, 6)),
            dma((2, NGROUP, 2, 6)),
            dma((NORB,)),
            dma((NORB,)),
            dma((2, max(1, len(RELAYED)))),
            dma((2, max(1, len(RELAYED)))),
            dma((NORB + 1,)),
        ],
        compiler_params=pltpu.CompilerParams(
            collective_id=0, has_side_effects=True, vmem_limit_bytes=62 * 1024 * 1024
        ),
    )(
        orbitals,
        potential,
        projectors.reshape(-1, projectors.shape[2]),
        entry_atom.reshape(1, -1),
        entry_block.reshape(1, -1),
        kb_energy.T,
        panel,
        *tables,
    )
    rows = HALF // XPARTS
    block = pl.BlockSpec((NORB, 1, rows, CZ), lambda h, x: (0, h, x, 0))
    return pl.pallas_call(
        rotate,
        grid=(2, XPARTS),
        out_shape=jax.ShapeDtypeStruct((1, NORB, CX, CY, CZ), F32),
        in_specs=[block, block, pl.BlockSpec((CZ, 2 * CZ), lambda h, x: (0, 0))],
        out_specs=pl.BlockSpec((1, NORB, CX // XPARTS, 8, CZ), lambda h, x: (0, 0, x, h, 0)),
    )(own, partner, mix)


def solution(mesh):
    in_specs = (
        P("dom", "band", None, None, None),
        P("dom", None, None, None),
        P("dom", None, None),
        P("dom"),
        P("dom"),
        P(),
        P(),
    )
    out_specs = P("dom", "band", None, None, None)
    return jax.shard_map(shards, mesh=mesh, in_specs=in_specs, out_specs=out_specs, check_vma=False)
```

```python
import jax
import jax.numpy as jnp
import ml_dtypes
import numpy as np
from jax import lax
from jax.experimental import pallas as pl
from jax.experimental.pallas import tpu as pltpu
from jax.sharding import PartitionSpec as P

COEFFS = (
    -5369.0 / 1800.0,
    12.0 / 7.0,
    -15.0 / 56.0,
    10.0 / 189.0,
    -1.0 / 112.0,
    2.0 / 1925.0,
    -1.0 / 16632.0,
)
KINETIC = -3.125
CENTER = 36.0
HALF_WIDTH = 34.0
REACH = 6

DOM_Z = 4
DOM_Y = 8
NORB = 8
CX, CY, CZ = 12, 16, 128
ENT = 256
ROWS = CX * CY
HALF = ROWS // 2
OWNED = 4
CHUNK = 2
NCHUNK = NORB // CHUNK
GROUP = 4
NGROUP = NORB // GROUP
MID_Y = DOM_Y // 2
RELAYED = (0, 1) if MID_Y > 1 else ()
LANE_SLOT = 16
SCALE = 64 * 1.0937445
F32 = jnp.float32
BF16 = jnp.bfloat16
OPPOSITE = (1, 0, 3, 2, 5, 4)
NN = (((1,), (0,)), ((), ()))
NT = (((1,), (1,)), ((), ()))


def tap(distance):
    return SCALE * COEFFS[abs(distance)]


def stencil_tables():
    plane = np.zeros((ROWS, 8 * HALF), np.float32)
    for x in range(CX):
        for y in range(CY):
            row = y // 8 * HALF + x * 8 + y % 8
            for step in (s for s in range(-REACH, REACH + 1) if s):
                to = x + step
                if 0 <= to < CX:
                    near = y // 8 * HALF + to * 8 + y % 8
                    plane[row, near] += tap(step)
                    plane[row, 6 * HALF + near] += tap(step)
                else:
                    place = (to + REACH) * 8 if to < 0 else HALF // 2 + (to - CX) * 8
                    plane[row, (2 + y // 8) * HALF + place + y % 8] += tap(step)
                to = y + step
                if 0 <= to < CY:
                    near = to // 8 * HALF + x * 8 + to % 8
                    plane[row, near] += tap(step)
                    plane[row, 6 * HALF + near] += tap(step)
                elif to < 0:
                    plane[row, 4 * HALF + x * 8 + to + 8] += tap(step)
                else:
                    plane[row, 5 * HALF + x * 8 + to - CY] += tap(step)
    line = np.zeros((2 * CZ, CZ), np.float32)
    edge = np.zeros((NORB, 2 * CZ, CZ), np.float32)
    pack = np.zeros((NORB, CZ, 2 * CZ), np.float32)
    for z in range(CZ):
        for step in (s for s in range(-REACH, REACH + 1) if s):
            to = z + step
            for o in range(NORB):
                if to < 0:
                    edge[o, o * LANE_SLOT + to + REACH, z] = tap(step)
                elif to >= CZ:
                    edge[o, CZ + o * LANE_SLOT + to - CZ, z] = tap(step)
            if 0 <= to < CZ:
                line[to, z] = line[CZ + to, z] = tap(step)
    for o in range(NORB):
        for k in range(REACH):
            pack[o, k, o * LANE_SLOT + k] = 1.0
            pack[o, CZ - REACH + k, CZ + o * LANE_SLOT + k] = 1.0
    return [t.astype(ml_dtypes.bfloat16) for t in (plane, line, edge, pack)]


def dot(a, b, dims=NN):
    return lax.dot_general(a, b, dims, preferred_element_type=F32)


def iota(shape, axis):
    return lax.broadcasted_iota(jnp.int32, shape, axis)


def split(values):
    high = values.astype(BF16)
    return high, (values - high.astype(F32)).astype(BF16)


def kernel(
    orb_hbm, pot_hbm, proj_hbm, atom_ref, block_ref, energy_hbm, panel_ref, plane_hbm, line_hbm, edge_hbm, pack_hbm,
    out,
    start, field, first, weight, proj, energy, plane, line, edge, pack,
    z_out, z_in, filtered, partner,
    pick, spread, slots, picked, inner, additions, table_out, table_in, scaled_out, scaled_in, mix, relay_in,
    local_sem, halo_send, halo_recv, table_send, table_recv, band_send, band_recv, relay_send, relay_recv,
):
    dom = lax.axis_index("dom")
    band = lax.axis_index("band")
    count = lax.axis_size("dom")
    plane_size = DOM_Y * DOM_Z
    at = (dom // plane_size, dom // DOM_Z % DOM_Y, dom % DOM_Z)
    extents = (count // plane_size, DOM_Y, DOM_Z)
    strides = (plane_size, -plane_size, DOM_Z, -DOM_Z, 1, -1)
    has = []
    for axis in range(3):
        has.append(at[axis] < extents[axis] - 1)
        has.append(at[axis] > 0)

    def toward(d):
        return {"dom": jnp.clip(dom + strides[d], 0, count - 1)}

    def away(offset):
        return {"dom": jnp.clip(dom + offset * DOM_Z, 0, count - 1)}

    relay_pairs = (
        (0, (MID_Y - 1, MID_Y)),
        (MID_Y - 1, (1 - MID_Y, MID_Y)),
        (MID_Y, (MID_Y - 1, -MID_Y)),
        (DOM_Y - 1, (1 - MID_Y, -MID_Y)),
    )
    routes = {
        2: (MID_Y - 1, 1 - MID_Y, 0, MID_Y),
        3: (MID_Y, MID_Y - 1, DOM_Y - 1, -MID_Y),
    }

    barrier = pltpu.get_barrier_semaphore()
    partners = jnp.int32(1)
    for d in range(6):
        partners = partners + has[d].astype(jnp.int32)

        @pl.when(has[d])
        def _():
            pl.semaphore_signal(barrier, inc=1, device_id=toward(d), device_id_type=pl.DeviceIdType.MESH)

    pl.semaphore_signal(barrier, inc=1, device_id={"band": 1 - band}, device_id_type=pl.DeviceIdType.MESH)
    for place, offsets in relay_pairs if RELAYED else ():
        partners = partners + jnp.where(at[1] == place, 2, 0)

        @pl.when(at[1] == place)
        def _():
            for offset in offsets:
                pl.semaphore_signal(
                    barrier, inc=1, device_id=away(offset), device_id_type=pl.DeviceIdType.MESH
                )

    loads = []

    def load(src, dst):
        copy = pltpu.make_async_copy(src, dst, local_sem.at[len(loads)])
        copy.start()
        loads.append(copy)
        return copy

    orb_loads = [
        [
            load(
                orb_hbm.at[0, pl.ds(c * CHUNK, CHUNK), :, pl.ds(h * 8, 8), :],
                start.at[pl.ds(c * CHUNK, CHUNK), h],
            )
            for h in range(2)
        ]
        for c in range(NCHUNK)
    ]
    pack_load = load(pack_hbm, pack)
    proj_load = load(proj_hbm, proj)
    pot_loads = [load(pot_hbm.at[0, :, pl.ds(h * 8, 8), :], weight.at[h]) for h in range(2)]
    width = energy.shape[1]
    energy_load = load(energy_hbm.at[:, pl.ds(pl.multiple_of(dom * OWNED // width * width, width), width)], energy)
    plane_load = load(plane_hbm, plane)
    line_load = load(line_hbm, line)
    edge_load = load(edge_hbm, edge)

    for h in range(2):
        for d in range(6):

            @pl.when(jnp.logical_not(has[OPPOSITE[d]]))
            def _():
                if d == 0:
                    field[h, :, 2:4, 0 : HALF // 2, :] = jnp.zeros((NORB, 2, HALF // 2, CZ), BF16)
                elif d == 1:
                    field[h, :, 2:4, HALF // 2 : HALF, :] = jnp.zeros((NORB, 2, HALF // 2, CZ), BF16)
                elif d == 2:
                    field[h, :, 4, :, :] = jnp.zeros((NORB, HALF, CZ), BF16)
                elif d == 3:
                    field[h, :, 5, :, :] = jnp.zeros((NORB, HALF, CZ), BF16)
                else:
                    z_in[h, :, d - 4] = jnp.zeros((NCHUNK, ROWS, CZ), BF16)
                table_in[h, d] = jnp.zeros((NGROUP, 8, CZ), F32)
                scaled_in[h, d] = jnp.zeros((NGROUP, 8, CZ), F32)

    table_out[...] = jnp.zeros(table_out.shape, F32)

    def halo(h, c, d):
        own = pl.ds(c * CHUNK, CHUNK)
        low, high = pl.ds(0, HALF // 2), pl.ds(HALF // 2, HALF // 2)
        if d == 0:
            src, dst = field.at[h, own, 0:2, high, :], field.at[h, own, 2:4, low, :]
        elif d == 1:
            src, dst = field.at[h, own, 0:2, low, :], field.at[h, own, 2:4, high, :]
        elif d == 2:
            src, dst = field.at[h, own, 1], field.at[h, own, 4]
        elif d == 3:
            src, dst = field.at[h, own, 0], field.at[h, own, 5]
        elif d == 4:
            src, dst = z_out.at[h, c, 1], z_in.at[h, c, 0]
        else:
            src, dst = z_out.at[h, c, 0], z_in.at[h, c, 1]
        return pltpu.make_async_remote_copy(
            src_ref=src,
            dst_ref=dst,
            send_sem=halo_send.at[h, c, d],
            recv_sem=halo_recv.at[h, c, d],
            device_id=toward(d),
            device_id_type=pl.DeviceIdType.MESH,
        )

    def to_relay(h, c, d):
        return pltpu.make_async_remote_copy(
            src_ref=field.at[h, pl.ds(c * CHUNK, CHUNK), 3 - d],
            dst_ref=relay_in.at[h, RELAYED.index(c)],
            send_sem=halo_send.at[h, c, d],
            recv_sem=relay_recv.at[h, RELAYED.index(c)],
            device_id=away(routes[d][1]),
            device_id_type=pl.DeviceIdType.MESH,
        )

    def from_relay(h, c, d):
        return pltpu.make_async_remote_copy(
            src_ref=relay_in.at[h, RELAYED.index(c)],
            dst_ref=field.at[h, pl.ds(c * CHUNK, CHUNK), 2 + d],
            send_sem=relay_send.at[h, RELAYED.index(c)],
            recv_sem=halo_recv.at[h, c, d],
            device_id=away(routes[d][3]),
            device_id_type=pl.DeviceIdType.MESH,
        )

    def forward(h, c):
        for d in routes if c in RELAYED else ():

            @pl.when(at[1] == routes[d][2])
            def _():
                to_relay(h, c, d).wait_recv()
                from_relay(h, c, d).start()

    def table(h, gs, kind, d):
        return pltpu.make_async_remote_copy(
            src_ref=(table_out, scaled_out)[kind].at[h, pl.ds(gs[0], len(gs))],
            dst_ref=(table_in, scaled_in)[kind].at[h, d, pl.ds(gs[0], len(gs))],
            send_sem=table_send.at[h, gs[0], kind, d],
            recv_sem=table_recv.at[h, gs[0], kind, d],
            device_id=toward(d),
            device_id_type=pl.DeviceIdType.MESH,
        )

    def exchange(o):
        return pltpu.make_async_remote_copy(
            src_ref=filtered.at[o],
            dst_ref=partner.at[o],
            send_sem=band_send.at[o],
            recv_sem=band_recv.at[o],
            device_id={"band": 1 - band},
            device_id_type=pl.DeviceIdType.MESH,
        )

    def start_all(make):
        for d in range(6):

            @pl.when(has[d])
            def _():
                make(d).start()

    def wait_recv_all(make):
        for d in range(6):

            @pl.when(has[OPPOSITE[d]])
            def _():
                make(d).wait_recv()

    def wait_send_all(make):
        for d in range(6):

            @pl.when(has[d])
            def _():
                make(d).wait_send()

    def high_of(h, o):
        return field[h, o, 0:2].reshape(ROWS, CZ)

    def low_of(h, o):
        return field[h, o, 6:8].reshape(ROWS, CZ)

    def keep(h, o, values):
        high, low = split(values.reshape(2, HALF, CZ))
        field[h, o, 0:2] = high
        field[h, o, 6:8] = low

    def send_halos(h, c):
        ends = None
        for o in range(c * CHUNK, (c + 1) * CHUNK):
            part = dot(high_of(h, o), pack[o])
            ends = part if ends is None else ends + part
        z_out[h, c, 0] = ends[:, :CZ].astype(BF16)
        z_out[h, c, 1] = ends[:, CZ:].astype(BF16)
        for d in range(6):
            direct = has[d]
            if d in routes and c in RELAYED:
                direct = jnp.logical_and(direct, at[1] != routes[d][0])

                @pl.when(at[1] == routes[d][0])
                def _():
                    to_relay(h, c, d).start()

            @pl.when(direct)
            def _():
                halo(h, c, d).start()

    for c in range(NCHUNK):
        for copy in orb_loads[c]:
            copy.wait()
        for o in range(c * CHUNK, (c + 1) * CHUNK):
            keep(0, o, start[o].reshape(ROWS, CZ))
        if c == 0:
            pack_load.wait()
            pl.semaphore_wait(barrier, partners)
            send_halos(0, c)

    every = tuple(range(NGROUP))

    proj_load.wait()
    mask = iota((32, CZ), 0) == iota((32, CZ), 1) // 4
    block = block_ref[...]
    row = ((block % 16) // 8) * HALF + (block // 16) * 8 + block % 8
    one_hot = (iota((ROWS, ENT), 0) == row).astype(F32).astype(BF16)
    spread[:, :ENT] = one_hot
    spread[:, ENT:] = one_hot
    diagonal = iota((ENT, ENT), 0) == iota((ENT, ENT), 1)
    row_column = jnp.sum(jnp.where(diagonal, row.astype(F32), 0.0), axis=1, keepdims=True)
    pick[...] = (iota((ENT, ROWS), 1).astype(F32) == row_column).astype(F32).astype(BF16)
    atom = atom_ref[...]
    gap = atom // OWNED - dom
    slot = jnp.zeros_like(gap)
    for d in range(6):
        slot = jnp.where(gap == strides[d], d + 1, slot)
    code = (slot * OWNED + atom % OWNED).astype(F32)
    code_column = jnp.sum(jnp.where(diagonal, code, 0.0), axis=1, keepdims=True)
    for q in range(8):
        lanes = jnp.sum(jnp.where(mask, code_column[q * 32 : (q + 1) * 32], 0.0), axis=0, keepdims=True)
        wanted = lanes * 4.0 + (iota((1, CZ), 1) % 4).astype(F32)
        slots[:, q * CZ : (q + 1) * CZ] = (iota((CZ, CZ), 0).astype(F32) == wanted).astype(F32).astype(BF16)

    energy_load.wait()
    here = dom * OWNED % width + iota((width, CZ), 1) // 4
    chosen = jnp.logical_and(iota((width, CZ), 0) == here, iota((width, CZ), 1) < 4 * OWNED)
    chosen = chosen.astype(F32).astype(BF16)
    high, low = split(energy[...])
    levels = dot(high, chosen) + dot(low, chosen)
    levels = jnp.where(iota((4, CZ), 1) % 4 == iota((4, CZ), 0), levels, 0.0)
    own_energy = jnp.sum(levels, axis=0, keepdims=True) * (SCALE / KINETIC)

    def project(h, g):
        for i in range(GROUP):
            o = g * GROUP + i
            both = jnp.concatenate([high_of(h, o), low_of(h, o)], axis=1)
            picked[:, i] = dot(pick[...], both).astype(BF16).reshape(8, 32, 2 * CZ)
        for q in range(8):
            values = proj[q * CZ : (q + 1) * CZ, :]
            pairs = dot(picked[q].reshape(GROUP * 32, 2 * CZ), jnp.concatenate([values, values], axis=1), NT)
            kept = jnp.where(mask.reshape(1, 4, 8, CZ), pairs.reshape(GROUP, 4, 8, CZ), 0.0)
            inner[:, q * CZ : (q + 1) * CZ] = jnp.sum(kept, axis=1).reshape(GROUP * 8, CZ)
        high, low = split(inner[...])
        sums = dot(jnp.concatenate([high, low], axis=0), slots[...], NT).reshape(2, GROUP, 8, CZ)
        table_out[h, g, 0:GROUP] = jnp.sum(jnp.sum(sums, axis=0), axis=1)

    def send_sums(h, gs):
        start_all(lambda d: table(h, gs, 0, d))

    def scale_sums(h, gs):
        wait_recv_all(lambda d: table(h, gs, 0, d))
        for g in gs:
            total = table_out[h, g]
            for d in range(6):
                total = total + pltpu.roll(table_in[h, d, g], CZ - LANE_SLOT * (d + 1), 1)
            scaled_out[h, g] = jnp.where(iota((8, CZ), 1) < LANE_SLOT, total * own_energy, 0.0)
        start_all(lambda d: table(h, gs, 1, d))

    def wait_scaled(h, gs):
        wait_recv_all(lambda d: table(h, gs, 1, d))

    def add_projectors(h, g):
        scaled = scaled_out[h, g]
        for d in range(6):
            scaled = scaled + pltpu.roll(scaled_in[h, d, g], LANE_SLOT * (OPPOSITE[d] + 1), 1)
        high, low = split(scaled)
        entries = dot(jnp.concatenate([high, low], axis=0), slots[...])
        for q in range(8):
            lanes = slice(q * CZ, (q + 1) * CZ)
            rows = []
            for i in range(GROUP):
                rows.append(
                    jnp.concatenate(
                        [
                            jnp.where(mask, entries[i : i + 1, lanes], 0.0).astype(BF16),
                            jnp.where(mask, entries[8 + i : 9 + i, lanes], 0.0).astype(BF16),
                        ],
                        axis=1,
                    )
                )
            values = proj[lanes, :]
            added = dot(jnp.concatenate(rows, axis=0), jnp.concatenate([values, values], axis=0))
            high, low = split(added.reshape(GROUP, 32, CZ))
            additions[g * GROUP : (g + 1) * GROUP, 0, q * 32 : (q + 1) * 32] = high
            additions[g * GROUP : (g + 1) * GROUP, 1, q * 32 : (q + 1) * 32] = low

    def applied(h, c, o):
        total = dot(plane[...], field[h, o].reshape(8 * HALF, CZ))
        total = total + dot(jnp.concatenate([high_of(h, o), low_of(h, o)], axis=1), line[...])
        total = total + dot(jnp.concatenate([z_in[h, c, 0], z_in[h, c, 1]], axis=1), edge[o])
        return total + dot(spread[...], additions[o].reshape(2 * ENT, CZ))

    for g in range(NGROUP):
        project(0, g)
    send_sums(0, every)
    send_halos(0, 1)
    send_halos(0, 2)

    jj = iota((CZ, 16), 0) // 16 + band * NORB
    choose_out = (iota((CZ, 16), 1) == jj).astype(F32).astype(BF16)
    column = iota((16, 2 * CZ), 1) // 16
    own = column < NORB
    wanted = jnp.where(own, column + band * NORB, column - NORB + (1 - band) * NORB)
    choose_in = (iota((16, 2 * CZ), 0) == wanted).astype(F32).astype(BF16)
    rows_of = dot(choose_out, panel_ref[...], NT).astype(BF16)
    spread_panel = dot(rows_of, choose_in)
    same = iota((CZ, 2 * CZ), 0) % 16 == iota((CZ, 2 * CZ), 1) % 16
    mix[...] = jnp.where(same, spread_panel, 0.0).astype(BF16)

    for copy in pot_loads:
        copy.wait()
    center = KINETIC * 3.0 * COEFFS[0] - CENTER
    weight[...] = (weight[...] + center) * (1.0 / HALF_WIDTH)
    slope = KINETIC / (SCALE * HALF_WIDTH)

    scale_sums(0, every)
    forward(0, 0)
    send_halos(0, 3)
    forward(0, 1)
    wait_scaled(0, every)
    for g in every:
        add_projectors(0, g)
    plane_load.wait()
    line_load.wait()
    edge_load.wait()

    def first_chunk(c):
        wait_recv_all(lambda d: halo(0, c, d))
        for o in range(c * CHUNK, (c + 1) * CHUNK):
            base = weight[...].reshape(ROWS, CZ) * start[o].reshape(ROWS, CZ)
            values = slope * applied(0, c, o) + base
            first[o] = values
            keep(1, o, values)

    def second_chunk(c):
        wait_recv_all(lambda d: halo(1, c, d))
        for o in range(c * CHUNK, (c + 1) * CHUNK):
            base = weight[...].reshape(ROWS, CZ) * first[o]
            values = 2.0 * (slope * applied(1, c, o) + base) - start[o].reshape(ROWS, CZ)
            filtered[o] = values.astype(BF16).reshape(2, HALF, CZ)
            exchange(o).start()

    first_chunk(0)
    send_halos(1, 0)
    first_chunk(1)
    project(1, 0)
    send_sums(1, (0,))
    send_halos(1, 1)
    first_chunk(2)
    first_chunk(3)
    project(1, 1)
    send_sums(1, (1,))
    scale_sums(1, (0,))
    forward(1, 0)
    send_halos(1, 2)
    forward(1, 1)
    scale_sums(1, (1,))
    send_halos(1, 3)
    wait_scaled(1, (0,))
    add_projectors(1, 0)
    second_chunk(0)
    second_chunk(1)
    wait_scaled(1, (1,))
    add_projectors(1, 1)
    second_chunk(2)
    second_chunk(3)

    for o in range(NORB):
        exchange(o).wait_recv()
    for h in range(2):
        for part in range(6):
            rows = slice(part * 16, (part + 1) * 16)
            cells = jnp.concatenate(
                [filtered[:, h, rows].reshape(CZ, CZ), partner[:, h, rows].reshape(CZ, CZ)], axis=0
            )
            out[0, :, 2 * part : 2 * part + 2, h * 8 : h * 8 + 8] = dot(mix[...], cells).reshape(NORB, 2, 8, CZ)

    for o in range(NORB):
        exchange(o).wait_send()
    for h in range(2):
        for c in range(NCHUNK):
            wait_send_all(lambda d: halo(h, c, d))
        for gs in (every,) if h == 0 else tuple((g,) for g in every):
            for kind in range(2):
                wait_send_all(lambda d: table(h, gs, kind, d))
        for c in RELAYED:
            for d in routes:

                @pl.when(at[1] == routes[d][2])
                def _():
                    from_relay(h, c, d).wait_send()


def shards(orbitals, potential, projectors, entry_atom, entry_block, kb_energy, panel):
    tables = [jnp.asarray(t) for t in stencil_tables()]
    anywhere = pl.BlockSpec(memory_space=pltpu.HBM)
    vmem = pl.BlockSpec(memory_space=pltpu.VMEM)
    dma = pltpu.SemaphoreType.DMA
    return pl.pallas_call(
        kernel,
        out_shape=pltpu.VMEM((1, NORB, CX, CY, CZ), F32),
        in_specs=[anywhere, anywhere, anywhere, vmem, vmem, anywhere, vmem] + [anywhere] * 4,
        out_specs=pl.BlockSpec(memory_space=pltpu.VMEM),
        scratch_shapes=[
            pltpu.VMEM((NORB, 2, CX, 8, CZ), F32),
            pltpu.VMEM((2, NORB, 8, HALF, CZ), BF16),
            pltpu.VMEM((NORB, ROWS, CZ), F32),
            pltpu.VMEM((2, CX, 8, CZ), F32),
            pltpu.VMEM((4 * ENT, CZ), BF16),
            pltpu.VMEM((4, min(128, kb_energy.shape[0])), F32),
            pltpu.VMEM((ROWS, 8 * HALF), BF16),
            pltpu.VMEM((2 * CZ, CZ), BF16),
            pltpu.VMEM((NORB, 2 * CZ, CZ), BF16),
            pltpu.VMEM((NORB, CZ, 2 * CZ), BF16),
            pltpu.VMEM((2, NCHUNK, 2, ROWS, CZ), BF16),
            pltpu.VMEM((2, NCHUNK, 2, ROWS, CZ), BF16),
            pltpu.VMEM((NORB, 2, HALF, CZ), BF16),
            pltpu.VMEM((NORB, 2, HALF, CZ), BF16),
            pltpu.VMEM((ENT, ROWS), BF16),
            pltpu.VMEM((ROWS, 2 * ENT), BF16),
            pltpu.VMEM((CZ, 4 * ENT), BF16),
            pltpu.VMEM((8, GROUP, 32, 2 * CZ), BF16),
            pltpu.VMEM((GROUP * 8, 4 * ENT), F32),
            pltpu.VMEM((NORB, 2, ENT, CZ), BF16),
            pltpu.VMEM((2, NGROUP, 8, CZ), F32),
            pltpu.VMEM((2, 6, NGROUP, 8, CZ), F32),
            pltpu.VMEM((2, NGROUP, 8, CZ), F32),
            pltpu.VMEM((2, 6, NGROUP, 8, CZ), F32),
            pltpu.VMEM((CZ, 2 * CZ), BF16),
            pltpu.VMEM((2, max(1, len(RELAYED)), CHUNK, HALF, CZ), BF16),
            dma((2 * NCHUNK + 8,)),
            dma((2, NCHUNK, 6)),
            dma((2, NCHUNK, 6)),
            dma((2, NGROUP, 2, 6)),
            dma((2, NGROUP, 2, 6)),
            dma((NORB,)),
            dma((NORB,)),
            dma((2, max(1, len(RELAYED)))),
            dma((2, max(1, len(RELAYED)))),
        ],
        compiler_params=pltpu.CompilerParams(
            collective_id=0, has_side_effects=True, vmem_limit_bytes=62 * 1024 * 1024
        ),
    )(
        orbitals,
        potential,
        projectors.reshape(-1, projectors.shape[2]),
        entry_atom.reshape(1, -1),
        entry_block.reshape(1, -1),
        kb_energy.T,
        panel,
        *tables,
    )


def solution(mesh):
    in_specs = (
        P("dom", "band", None, None, None),
        P("dom", None, None, None),
        P("dom", None, None),
        P("dom"),
        P("dom"),
        P(),
        P(),
    )
    out_specs = P("dom", "band", None, None, None)
    return jax.shard_map(shards, mesh=mesh, in_specs=in_specs, out_specs=out_specs, check_vma=False)
```

```python
import jax
import jax.numpy as jnp
import ml_dtypes
import numpy as np
from jax import lax
from jax.experimental import pallas as pl
from jax.experimental.pallas import tpu as pltpu
from jax.sharding import PartitionSpec as P

COEFFS = (
    -5369.0 / 1800.0,
    12.0 / 7.0,
    -15.0 / 56.0,
    10.0 / 189.0,
    -1.0 / 112.0,
    2.0 / 1925.0,
    -1.0 / 16632.0,
)
KINETIC = -3.125
CENTER = 36.0
HALF_WIDTH = 34.0
REACH = 6

DOM_Z = 4
DOM_Y = 8
NORB = 8
CX, CY, CZ = 12, 16, 128
ENT = 256
ROWS = CX * CY
HALF = ROWS // 2
OWNED = 4
CHUNK = 2
NCHUNK = NORB // CHUNK
GROUP = 4
NGROUP = NORB // GROUP
MID_Y = DOM_Y // 2
RELAYED = (0, 1) if MID_Y > 1 else ()
LANE_SLOT = 16
SCALE = 64 * 1.0937445
F32 = jnp.float32
BF16 = jnp.bfloat16
OPPOSITE = (1, 0, 3, 2, 5, 4)
NN = (((1,), (0,)), ((), ()))
NT = (((1,), (1,)), ((), ()))


def tap(distance):
    return SCALE * COEFFS[abs(distance)]


def stencil_tables():
    plane = np.zeros((ROWS, 8 * HALF), np.float32)
    for x in range(CX):
        for y in range(CY):
            row = y // 8 * HALF + x * 8 + y % 8
            for step in (s for s in range(-REACH, REACH + 1) if s):
                to = x + step
                if 0 <= to < CX:
                    near = y // 8 * HALF + to * 8 + y % 8
                    plane[row, near] += tap(step)
                    plane[row, 6 * HALF + near] += tap(step)
                else:
                    place = (to + REACH) * 8 if to < 0 else HALF // 2 + (to - CX) * 8
                    plane[row, (2 + y // 8) * HALF + place + y % 8] += tap(step)
                to = y + step
                if 0 <= to < CY:
                    near = to // 8 * HALF + x * 8 + to % 8
                    plane[row, near] += tap(step)
                    plane[row, 6 * HALF + near] += tap(step)
                elif to < 0:
                    plane[row, 4 * HALF + x * 8 + to + 8] += tap(step)
                else:
                    plane[row, 5 * HALF + x * 8 + to - CY] += tap(step)
    line = np.zeros((2 * CZ, CZ), np.float32)
    edge = np.zeros((NORB, 2 * CZ, CZ), np.float32)
    pack = np.zeros((NORB, CZ, 2 * CZ), np.float32)
    for z in range(CZ):
        for step in (s for s in range(-REACH, REACH + 1) if s):
            to = z + step
            for o in range(NORB):
                if to < 0:
                    edge[o, o * LANE_SLOT + to + REACH, z] = tap(step)
                elif to >= CZ:
                    edge[o, CZ + o * LANE_SLOT + to - CZ, z] = tap(step)
            if 0 <= to < CZ:
                line[to, z] = line[CZ + to, z] = tap(step)
    for o in range(NORB):
        for k in range(REACH):
            pack[o, k, o * LANE_SLOT + k] = 1.0
            pack[o, CZ - REACH + k, CZ + o * LANE_SLOT + k] = 1.0
    return [t.astype(ml_dtypes.bfloat16) for t in (plane, line, edge, pack)]


def dot(a, b, dims=NN):
    return lax.dot_general(a, b, dims, preferred_element_type=F32)


def iota(shape, axis):
    return lax.broadcasted_iota(jnp.int32, shape, axis)


def split(values):
    high = values.astype(BF16)
    return high, (values - high.astype(F32)).astype(BF16)


def kernel(
    orb_hbm, pot_hbm, proj_hbm, atom_ref, block_ref, energy_hbm, panel_ref, plane_hbm, line_hbm, edge_hbm, pack_hbm,
    out,
    start, field, first, weight, proj, energy, plane, line, edge, pack,
    z_out, z_in, filtered, partner,
    pick, spread, slots, picked, inner, additions, table_out, table_in, scaled_out, scaled_in, mix, relay_in,
    local_sem, halo_send, halo_recv, table_send, table_recv, band_send, band_recv, relay_send, relay_recv,
):
    dom = lax.axis_index("dom")
    band = lax.axis_index("band")
    count = lax.axis_size("dom")
    plane_size = DOM_Y * DOM_Z
    at = (dom // plane_size, dom // DOM_Z % DOM_Y, dom % DOM_Z)
    extents = (count // plane_size, DOM_Y, DOM_Z)
    strides = (plane_size, -plane_size, DOM_Z, -DOM_Z, 1, -1)
    has = []
    for axis in range(3):
        has.append(at[axis] < extents[axis] - 1)
        has.append(at[axis] > 0)

    def toward(d):
        return {"dom": jnp.clip(dom + strides[d], 0, count - 1)}

    def away(offset):
        return {"dom": jnp.clip(dom + offset * DOM_Z, 0, count - 1)}

    relay_pairs = (
        (0, (MID_Y - 1, MID_Y)),
        (MID_Y - 1, (1 - MID_Y, MID_Y)),
        (MID_Y, (MID_Y - 1, -MID_Y)),
        (DOM_Y - 1, (1 - MID_Y, -MID_Y)),
    )
    routes = {
        2: (MID_Y - 1, 1 - MID_Y, 0, MID_Y),
        3: (MID_Y, MID_Y - 1, DOM_Y - 1, -MID_Y),
    }

    barrier = pltpu.get_barrier_semaphore()
    partners = jnp.int32(1)
    for d in range(6):
        partners = partners + has[d].astype(jnp.int32)

        @pl.when(has[d])
        def _():
            pl.semaphore_signal(barrier, inc=1, device_id=toward(d), device_id_type=pl.DeviceIdType.MESH)

    pl.semaphore_signal(barrier, inc=1, device_id={"band": 1 - band}, device_id_type=pl.DeviceIdType.MESH)
    for place, offsets in relay_pairs if RELAYED else ():
        partners = partners + jnp.where(at[1] == place, 2, 0)

        @pl.when(at[1] == place)
        def _():
            for offset in offsets:
                pl.semaphore_signal(
                    barrier, inc=1, device_id=away(offset), device_id_type=pl.DeviceIdType.MESH
                )

    loads = []

    def load(src, dst):
        copy = pltpu.make_async_copy(src, dst, local_sem.at[len(loads)])
        copy.start()
        loads.append(copy)
        return copy

    orb_loads = [
        [
            load(
                orb_hbm.at[0, pl.ds(c * CHUNK, CHUNK), :, pl.ds(h * 8, 8), :],
                start.at[pl.ds(c * CHUNK, CHUNK), h],
            )
            for h in range(2)
        ]
        for c in range(NCHUNK)
    ]
    pack_load = load(pack_hbm, pack)
    proj_load = load(proj_hbm, proj)
    pot_loads = [load(pot_hbm.at[0, :, pl.ds(h * 8, 8), :], weight.at[h]) for h in range(2)]
    width = energy.shape[1]
    energy_load = load(energy_hbm.at[:, pl.ds(pl.multiple_of(dom * OWNED // width * width, width), width)], energy)
    plane_load = load(plane_hbm, plane)
    line_load = load(line_hbm, line)
    edge_load = load(edge_hbm, edge)

    for h in range(2):
        for d in range(6):

            @pl.when(jnp.logical_not(has[OPPOSITE[d]]))
            def _():
                if d == 0:
                    field[h, :, 2:4, 0 : HALF // 2, :] = jnp.zeros((NORB, 2, HALF // 2, CZ), BF16)
                elif d == 1:
                    field[h, :, 2:4, HALF // 2 : HALF, :] = jnp.zeros((NORB, 2, HALF // 2, CZ), BF16)
                elif d == 2:
                    field[h, :, 4, :, :] = jnp.zeros((NORB, HALF, CZ), BF16)
                elif d == 3:
                    field[h, :, 5, :, :] = jnp.zeros((NORB, HALF, CZ), BF16)
                else:
                    z_in[h, :, d - 4] = jnp.zeros((NCHUNK, ROWS, CZ), BF16)
                table_in[h, d] = jnp.zeros((NGROUP, 8, CZ), F32)
                scaled_in[h, d] = jnp.zeros((NGROUP, 8, CZ), F32)

    table_out[...] = jnp.zeros(table_out.shape, F32)

    def halo(h, c, d):
        own = pl.ds(c * CHUNK, CHUNK)
        low, high = pl.ds(0, HALF // 2), pl.ds(HALF // 2, HALF // 2)
        if d == 0:
            src, dst = field.at[h, own, 0:2, high, :], field.at[h, own, 2:4, low, :]
        elif d == 1:
            src, dst = field.at[h, own, 0:2, low, :], field.at[h, own, 2:4, high, :]
        elif d == 2:
            src, dst = field.at[h, own, 1], field.at[h, own, 4]
        elif d == 3:
            src, dst = field.at[h, own, 0], field.at[h, own, 5]
        elif d == 4:
            src, dst = z_out.at[h, c, 1], z_in.at[h, c, 0]
        else:
            src, dst = z_out.at[h, c, 0], z_in.at[h, c, 1]
        return pltpu.make_async_remote_copy(
            src_ref=src,
            dst_ref=dst,
            send_sem=halo_send.at[h, c, d],
            recv_sem=halo_recv.at[h, c, d],
            device_id=toward(d),
            device_id_type=pl.DeviceIdType.MESH,
        )

    def to_relay(h, c, d):
        return pltpu.make_async_remote_copy(
            src_ref=field.at[h, pl.ds(c * CHUNK, CHUNK), 3 - d],
            dst_ref=relay_in.at[h, RELAYED.index(c)],
            send_sem=halo_send.at[h, c, d],
            recv_sem=relay_recv.at[h, RELAYED.index(c)],
            device_id=away(routes[d][1]),
            device_id_type=pl.DeviceIdType.MESH,
        )

    def from_relay(h, c, d):
        return pltpu.make_async_remote_copy(
            src_ref=relay_in.at[h, RELAYED.index(c)],
            dst_ref=field.at[h, pl.ds(c * CHUNK, CHUNK), 2 + d],
            send_sem=relay_send.at[h, RELAYED.index(c)],
            recv_sem=halo_recv.at[h, c, d],
            device_id=away(routes[d][3]),
            device_id_type=pl.DeviceIdType.MESH,
        )

    def forward(h, c):
        for d in routes if c in RELAYED else ():

            @pl.when(at[1] == routes[d][2])
            def _():
                to_relay(h, c, d).wait_recv()
                from_relay(h, c, d).start()

    def table(h, gs, kind, d):
        return pltpu.make_async_remote_copy(
            src_ref=(table_out, scaled_out)[kind].at[h, pl.ds(gs[0], len(gs))],
            dst_ref=(table_in, scaled_in)[kind].at[h, d, pl.ds(gs[0], len(gs))],
            send_sem=table_send.at[h, gs[0], kind, d],
            recv_sem=table_recv.at[h, gs[0], kind, d],
            device_id=toward(d),
            device_id_type=pl.DeviceIdType.MESH,
        )

    def exchange(o):
        return pltpu.make_async_remote_copy(
            src_ref=filtered.at[o],
            dst_ref=partner.at[o],
            send_sem=band_send.at[o],
            recv_sem=band_recv.at[o],
            device_id={"band": 1 - band},
            device_id_type=pl.DeviceIdType.MESH,
        )

    def start_all(make):
        for d in range(6):

            @pl.when(has[d])
            def _():
                make(d).start()

    def wait_recv_all(make):
        for d in range(6):

            @pl.when(has[OPPOSITE[d]])
            def _():
                make(d).wait_recv()

    def wait_send_all(make):
        for d in range(6):

            @pl.when(has[d])
            def _():
                make(d).wait_send()

    def high_of(h, o):
        return field[h, o, 0:2].reshape(ROWS, CZ)

    def low_of(h, o):
        return field[h, o, 6:8].reshape(ROWS, CZ)

    def keep(h, o, values):
        high, low = split(values.reshape(2, HALF, CZ))
        field[h, o, 0:2] = high
        field[h, o, 6:8] = low

    def send_halos(h, c):
        for d in range(6):
            direct = has[d]
            if d == 4:
                ends = None
                for o in range(c * CHUNK, (c + 1) * CHUNK):
                    part = dot(high_of(h, o), pack[o])
                    ends = part if ends is None else ends + part
                z_out[h, c, 0] = ends[:, :CZ].astype(BF16)
                z_out[h, c, 1] = ends[:, CZ:].astype(BF16)
            if d in routes and c in RELAYED:
                direct = jnp.logical_and(direct, at[1] != routes[d][0])

                @pl.when(at[1] == routes[d][0])
                def _():
                    to_relay(h, c, d).start()

            @pl.when(direct)
            def _():
                halo(h, c, d).start()

    for c in range(NCHUNK):
        for copy in orb_loads[c]:
            copy.wait()
        for o in range(c * CHUNK, (c + 1) * CHUNK):
            keep(0, o, start[o].reshape(ROWS, CZ))
        if c == 0:
            pack_load.wait()
            pl.semaphore_wait(barrier, partners)
            send_halos(0, c)

    every = tuple(range(NGROUP))

    proj_load.wait()
    mask = iota((32, CZ), 0) == iota((32, CZ), 1) // 4
    block = block_ref[...]
    row = ((block % 16) // 8) * HALF + (block // 16) * 8 + block % 8
    one_hot = (iota((ROWS, ENT), 0) == row).astype(F32).astype(BF16)
    spread[:, :ENT] = one_hot
    spread[:, ENT:] = one_hot
    diagonal = iota((ENT, ENT), 0) == iota((ENT, ENT), 1)
    row_column = jnp.sum(jnp.where(diagonal, row.astype(F32), 0.0), axis=1, keepdims=True)
    pick[...] = (iota((ENT, ROWS), 1).astype(F32) == row_column).astype(F32).astype(BF16)
    atom = atom_ref[...]
    gap = atom // OWNED - dom
    slot = jnp.zeros_like(gap)
    for d in range(6):
        slot = jnp.where(gap == strides[d], d + 1, slot)
    code = (slot * OWNED + atom % OWNED).astype(F32)
    code_column = jnp.sum(jnp.where(diagonal, code, 0.0), axis=1, keepdims=True)
    for q in range(8):
        lanes = jnp.sum(jnp.where(mask, code_column[q * 32 : (q + 1) * 32], 0.0), axis=0, keepdims=True)
        wanted = lanes * 4.0 + (iota((1, CZ), 1) % 4).astype(F32)
        slots[:, q * CZ : (q + 1) * CZ] = (iota((CZ, CZ), 0).astype(F32) == wanted).astype(F32).astype(BF16)

    energy_load.wait()
    here = dom * OWNED % width + iota((width, CZ), 1) // 4
    chosen = jnp.logical_and(iota((width, CZ), 0) == here, iota((width, CZ), 1) < 4 * OWNED)
    chosen = chosen.astype(F32).astype(BF16)
    high, low = split(energy[...])
    levels = dot(high, chosen) + dot(low, chosen)
    levels = jnp.where(iota((4, CZ), 1) % 4 == iota((4, CZ), 0), levels, 0.0)
    own_energy = jnp.sum(levels, axis=0, keepdims=True) * (SCALE / KINETIC)

    def project(h, g):
        for i in range(GROUP):
            o = g * GROUP + i
            both = jnp.concatenate([high_of(h, o), low_of(h, o)], axis=1)
            picked[:, i] = dot(pick[...], both).astype(BF16).reshape(8, 32, 2 * CZ)
        for q in range(8):
            values = proj[q * CZ : (q + 1) * CZ, :]
            pairs = dot(picked[q].reshape(GROUP * 32, 2 * CZ), jnp.concatenate([values, values], axis=1), NT)
            kept = jnp.where(mask.reshape(1, 4, 8, CZ), pairs.reshape(GROUP, 4, 8, CZ), 0.0)
            inner[:, q * CZ : (q + 1) * CZ] = jnp.sum(kept, axis=1).reshape(GROUP * 8, CZ)
        high, low = split(inner[...])
        sums = dot(jnp.concatenate([high, low], axis=0), slots[...], NT).reshape(2, GROUP, 8, CZ)
        table_out[h, g, 0:GROUP] = jnp.sum(jnp.sum(sums, axis=0), axis=1)

    def send_sums(h, gs):
        start_all(lambda d: table(h, gs, 0, d))

    def scale_sums(h, gs):
        wait_recv_all(lambda d: table(h, gs, 0, d))
        for g in gs:
            total = table_out[h, g]
            for d in range(6):
                total = total + pltpu.roll(table_in[h, d, g], CZ - LANE_SLOT * (d + 1), 1)
            scaled_out[h, g] = jnp.where(iota((8, CZ), 1) < LANE_SLOT, total * own_energy, 0.0)
        start_all(lambda d: table(h, gs, 1, d))

    def wait_scaled(h, gs):
        wait_recv_all(lambda d: table(h, gs, 1, d))

    def add_projectors(h, g):
        scaled = scaled_out[h, g]
        for d in range(6):
            scaled = scaled + pltpu.roll(scaled_in[h, d, g], LANE_SLOT * (OPPOSITE[d] + 1), 1)
        high, low = split(scaled)
        entries = dot(jnp.concatenate([high, low], axis=0), slots[...])
        for q in range(8):
            lanes = slice(q * CZ, (q + 1) * CZ)
            rows = []
            for i in range(GROUP):
                rows.append(
                    jnp.concatenate(
                        [
                            jnp.where(mask, entries[i : i + 1, lanes], 0.0).astype(BF16),
                            jnp.where(mask, entries[8 + i : 9 + i, lanes], 0.0).astype(BF16),
                        ],
                        axis=1,
                    )
                )
            values = proj[lanes, :]
            added = dot(jnp.concatenate(rows, axis=0), jnp.concatenate([values, values], axis=0))
            high, low = split(added.reshape(GROUP, 32, CZ))
            additions[g * GROUP : (g + 1) * GROUP, 0, q * 32 : (q + 1) * 32] = high
            additions[g * GROUP : (g + 1) * GROUP, 1, q * 32 : (q + 1) * 32] = low

    def applied(h, c, o):
        total = dot(plane[...], field[h, o].reshape(8 * HALF, CZ))
        total = total + dot(jnp.concatenate([high_of(h, o), low_of(h, o)], axis=1), line[...])
        total = total + dot(jnp.concatenate([z_in[h, c, 0], z_in[h, c, 1]], axis=1), edge[o])
        return total + dot(spread[...], additions[o].reshape(2 * ENT, CZ))

    for g in range(NGROUP):
        project(0, g)
    send_sums(0, every)
    send_halos(0, 1)
    send_halos(0, 2)

    jj = iota((CZ, 16), 0) // 16 + band * NORB
    choose_out = (iota((CZ, 16), 1) == jj).astype(F32).astype(BF16)
    column = iota((16, 2 * CZ), 1) // 16
    own = column < NORB
    wanted = jnp.where(own, column + band * NORB, column - NORB + (1 - band) * NORB)
    choose_in = (iota((16, 2 * CZ), 0) == wanted).astype(F32).astype(BF16)
    rows_of = dot(choose_out, panel_ref[...], NT).astype(BF16)
    spread_panel = dot(rows_of, choose_in)
    same = iota((CZ, 2 * CZ), 0) % 16 == iota((CZ, 2 * CZ), 1) % 16
    mix[...] = jnp.where(same, spread_panel, 0.0).astype(BF16)

    for copy in pot_loads:
        copy.wait()
    center = KINETIC * 3.0 * COEFFS[0] - CENTER
    weight[...] = (weight[...] + center) * (1.0 / HALF_WIDTH)
    slope = KINETIC / (SCALE * HALF_WIDTH)

    scale_sums(0, every)
    forward(0, 0)
    send_halos(0, 3)
    forward(0, 1)
    wait_scaled(0, every)
    for g in every:
        add_projectors(0, g)
    plane_load.wait()
    line_load.wait()
    edge_load.wait()

    def first_chunk(c):
        wait_recv_all(lambda d: halo(0, c, d))
        for o in range(c * CHUNK, (c + 1) * CHUNK):
            base = weight[...].reshape(ROWS, CZ) * start[o].reshape(ROWS, CZ)
            values = slope * applied(0, c, o) + base
            first[o] = values
            keep(1, o, values)

    def second_chunk(c):
        wait_recv_all(lambda d: halo(1, c, d))
        for o in range(c * CHUNK, (c + 1) * CHUNK):
            base = weight[...].reshape(ROWS, CZ) * first[o]
            values = 2.0 * (slope * applied(1, c, o) + base) - start[o].reshape(ROWS, CZ)
            filtered[o] = values.astype(BF16).reshape(2, HALF, CZ)
            exchange(o).start()

    first_chunk(0)
    send_halos(1, 0)
    first_chunk(1)
    project(1, 0)
    send_sums(1, (0,))
    send_halos(1, 1)
    first_chunk(2)
    first_chunk(3)
    project(1, 1)
    send_sums(1, (1,))
    scale_sums(1, (0,))
    forward(1, 0)
    send_halos(1, 2)
    forward(1, 1)
    scale_sums(1, (1,))
    send_halos(1, 3)
    wait_scaled(1, (0,))
    add_projectors(1, 0)
    second_chunk(0)
    second_chunk(1)
    wait_scaled(1, (1,))
    add_projectors(1, 1)
    second_chunk(2)
    second_chunk(3)

    def rotate(first_o, count_o, source, columns, add):
        for h in range(2):
            for part in range(6):
                rows = slice(part * 16, (part + 1) * 16)
                cells = source[first_o : first_o + count_o, h, rows].reshape(count_o * 16, CZ)
                value = dot(mix[:, columns : columns + count_o * 16], cells).reshape(NORB, 2, 8, CZ)
                place = (0, slice(None), slice(2 * part, 2 * part + 2), slice(h * 8, h * 8 + 8))
                out[place] = out[place] + value if add else value

    rotate(0, NORB, filtered, 0, False)
    for o in range(NORB):
        exchange(o).wait_recv()
    rotate(0, NORB, partner, CZ, True)

    for o in range(NORB):
        exchange(o).wait_send()
    for h in range(2):
        for c in range(NCHUNK):
            wait_send_all(lambda d: halo(h, c, d))
        for gs in (every,) if h == 0 else tuple((g,) for g in every):
            for kind in range(2):
                wait_send_all(lambda d: table(h, gs, kind, d))
        for c in RELAYED:
            for d in routes:

                @pl.when(at[1] == routes[d][2])
                def _():
                    from_relay(h, c, d).wait_send()


def shards(orbitals, potential, projectors, entry_atom, entry_block, kb_energy, panel):
    tables = [jnp.asarray(t) for t in stencil_tables()]
    anywhere = pl.BlockSpec(memory_space=pltpu.HBM)
    vmem = pl.BlockSpec(memory_space=pltpu.VMEM)
    dma = pltpu.SemaphoreType.DMA
    return pl.pallas_call(
        kernel,
        out_shape=pltpu.VMEM((1, NORB, CX, CY, CZ), F32),
        in_specs=[anywhere, anywhere, anywhere, vmem, vmem, anywhere, vmem] + [anywhere] * 4,
        out_specs=pl.BlockSpec(memory_space=pltpu.VMEM),
        scratch_shapes=[
            pltpu.VMEM((NORB, 2, CX, 8, CZ), F32),
            pltpu.VMEM((2, NORB, 8, HALF, CZ), BF16),
            pltpu.VMEM((NORB, ROWS, CZ), F32),
            pltpu.VMEM((2, CX, 8, CZ), F32),
            pltpu.VMEM((4 * ENT, CZ), BF16),
            pltpu.VMEM((4, min(128, kb_energy.shape[0])), F32),
            pltpu.VMEM((ROWS, 8 * HALF), BF16),
            pltpu.VMEM((2 * CZ, CZ), BF16),
            pltpu.VMEM((NORB, 2 * CZ, CZ), BF16),
            pltpu.VMEM((NORB, CZ, 2 * CZ), BF16),
            pltpu.VMEM((2, NCHUNK, 2, ROWS, CZ), BF16),
            pltpu.VMEM((2, NCHUNK, 2, ROWS, CZ), BF16),
            pltpu.VMEM((NORB, 2, HALF, CZ), BF16),
            pltpu.VMEM((NORB, 2, HALF, CZ), BF16),
            pltpu.VMEM((ENT, ROWS), BF16),
            pltpu.VMEM((ROWS, 2 * ENT), BF16),
            pltpu.VMEM((CZ, 4 * ENT), BF16),
            pltpu.VMEM((8, GROUP, 32, 2 * CZ), BF16),
            pltpu.VMEM((GROUP * 8, 4 * ENT), F32),
            pltpu.VMEM((NORB, 2, ENT, CZ), BF16),
            pltpu.VMEM((2, NGROUP, 8, CZ), F32),
            pltpu.VMEM((2, 6, NGROUP, 8, CZ), F32),
            pltpu.VMEM((2, NGROUP, 8, CZ), F32),
            pltpu.VMEM((2, 6, NGROUP, 8, CZ), F32),
            pltpu.VMEM((CZ, 2 * CZ), BF16),
            pltpu.VMEM((2, max(1, len(RELAYED)), CHUNK, HALF, CZ), BF16),
            dma((2 * NCHUNK + 8,)),
            dma((2, NCHUNK, 6)),
            dma((2, NCHUNK, 6)),
            dma((2, NGROUP, 2, 6)),
            dma((2, NGROUP, 2, 6)),
            dma((NORB,)),
            dma((NORB,)),
            dma((2, max(1, len(RELAYED)))),
            dma((2, max(1, len(RELAYED)))),
        ],
        compiler_params=pltpu.CompilerParams(
            collective_id=0, has_side_effects=True, vmem_limit_bytes=62 * 1024 * 1024
        ),
    )(
        orbitals,
        potential,
        projectors.reshape(-1, projectors.shape[2]),
        entry_atom.reshape(1, -1),
        entry_block.reshape(1, -1),
        kb_energy.T,
        panel,
        *tables,
    )


def solution(mesh):
    in_specs = (
        P("dom", "band", None, None, None),
        P("dom", None, None, None),
        P("dom", None, None),
        P("dom"),
        P("dom"),
        P(),
        P(),
    )
    out_specs = P("dom", "band", None, None, None)
    return jax.shard_map(shards, mesh=mesh, in_specs=in_specs, out_specs=out_specs, check_vma=False)
```
